512 devices in a mesh: tile: 128 (over y, z, core), spec: 4 (over x).
Axes of the slice: x: 4, y: 8, z: 8, core: 2. Of those that a mesh axis runs over, the one named last changes fastest.
Arguments:
- grad_columns: bfloat16 [131072, 512], P('tile', 'spec'), may hold values from -6 to 6
- grad_flux: float32 [16, 131072], P('spec', 'tile'), may hold values from -6 to 6
- remap_part: int32 [131072, 4], P('tile'), may hold values from 0 to 127, all different within a row; in each aligned block of 1024 rows (0 to 1023, 1024 to 2047, ...) at most 64 rows name the same one
- remap_slot: int32 [131072, 4], P('tile'), may hold values from 0 to 1023
- remap_weight: float32 [131072, 4], P('tile'), may hold values from 0.2 to 1
- col_count: int32 [128], P('tile'), may hold values from 341 to 1024, as said below
- neighbors: int32 [131072, 4], P('tile'), may hold values from 0 to 1279, as said below
- kappa: float32 [16], P('spec'), may hold values from 0.03 to 0.2
- thickness: float32 [16, 32], P('spec'), may hold values from 0.2 to 2
- vertical: bfloat16 [16, 32, 32], P('spec'), may hold values from -1 to 1
- reaction: bfloat16 [16, 16], P(None, 'spec'), may hold values from -1.5 to 1.5
Outputs:
- grad_state: bfloat16 [131072, 512], P('tile', 'spec')
- grad_bottom: float32 [16, 131072], P('spec', 'tile')
The draws below stay inside these ranges and needn't reach their ends.
Inputs may be any that keep to these rules, and one draw needn't show every extreme that they name: `remap_part`: each coarse cell names 4 different partitions; the entries of the cells of one tile (1024 cells) name one partition at most 64 times. `col_count`: live counts of partitions differ up to threefold; one partition holds 1024 live columns and one holds 341. `neighbors`: row p * 1024 + i lists the codes of 4 neighbours of slot i of partition p; every named slot is live; the first partition names no previous and the last no next partition.
All inputs are finite; a program needn't handle non-finite values.
Results may differ from the reference program's by a relative error of at most 0.008.
Values may be sent and summed in bfloat16 or wider, within the bound.
A program may use at most 128 MiB of HBM per device.

```python
import math
import jax
import jax.numpy as jnp
import numpy as np
from jax import lax

S = 16
L = 32
CMAX = 1024
CC = 1024
RB = 4
NB = 4
SUB = 4
HW = 128
PARTS_SIZE = 128
NF = 131072
NC = 131072
CAP = 64
N_TILE = 128


def count_helper(key):
    sub_key = jax.random.fold_in(key, 11)
    key_base, key_first, key_second = jax.random.split(sub_key, 3)
    counts = jax.random.randint(key_base, (PARTS_SIZE,), CMAX // 3, CMAX + 1)
    first_index = jax.random.randint(key_first, (), 0, PARTS_SIZE)
    second_index = (first_index + 1 + jax.random.randint(key_second, (), 0, PARTS_SIZE - 1)) % PARTS_SIZE
    counts = counts.at[first_index].set(CMAX).at[second_index].set(CMAX // 3)
    return counts.astype(jnp.int32)


def draw_col_count(key, part):
    return count_helper(key)


def draw_neighbors(key, part):
    counts = count_helper(key)
    offset_key = jax.random.fold_in(key, 23)
    offsets = jax.random.randint(offset_key, (PARTS_SIZE, CMAX, NB), -8, 9)
    slot_ids = jnp.arange(CMAX, dtype=jnp.int32)
    part_ids = jnp.arange(PARTS_SIZE, dtype=jnp.int32)
    own_codes = jnp.clip(slot_ids[None, :, None] + offsets, 0, counts[:, None, None] - 1)
    cross_prev = (slot_ids[None, :] < HW) & (part_ids[:, None] > 0)
    cross_next = (slot_ids[None, :] >= HW) & (slot_ids[None, :] < 2 * HW) & (part_ids[:, None] < PARTS_SIZE - 1)
    first_code = jnp.where(cross_prev | cross_next, CMAX + slot_ids[None, :], own_codes[:, :, 0])
    codes = own_codes.at[:, :, 0].set(first_code)
    return codes.reshape(PARTS_SIZE * CMAX, NB).astype(jnp.int32)


def set_ends(result, stream_key, least, top_value):
    spot = [jax.random.randint(jax.random.fold_in(stream_key, axis), (), 0, length) for axis, length in enumerate(result.shape)]
    widest = result.shape.index(max(result.shape))
    next_to = spot[:widest] + [(spot[widest] + 1) % result.shape[widest]] + spot[widest + 1:]
    return result.at[tuple(spot)].set(least).at[tuple(next_to)].set(top_value)


def block_levels(stream_key, dims, cuts, least, largest):
    def one(dim, parts):
        draws = jax.random.uniform(jax.random.fold_in(jax.random.fold_in(stream_key, 6), dim), (parts,), jnp.float32, least / len(cuts), largest / len(cuts))
        return jnp.repeat(jnp.exp(draws), dims[dim] // parts).reshape((-1,) + (1,) * (len(dims) - dim - 1))

    factor_of = one(*cuts[0])
    for cut in cuts[1:]:
        factor_of = factor_of * one(*cut)
    return factor_of


def shared_out(rng, own, number, rows, count, top, limit, slope):
    sequence = jax.random.permutation(rng, count)
    heavy_load, usual = load_shares(count, rows * top, limit, slope, True), load_shares(count, rows * top, limit, slope, False)
    places = jnp.arange(count)

    def named(tallies, offset_by):
        used = int((tallies > 0).sum())
        fixed = max(1, used // 4)
        moved = fixed + (places - fixed + offset_by * (used - fixed)) % max(1, count - fixed)
        return jnp.zeros((count,), jnp.int32).at[sequence[jnp.where(places < fixed, places, moved)]].set(jnp.asarray(tallies, jnp.int32))

    tallies = jnp.where(number % 4 == 0, named(heavy_load, number // 4), named(usual, number - number // 4 - 1))
    mixed = jax.random.permutation(jax.random.fold_in(own, 3), count)
    source_of, receiver = mixed[0:count // 2 * 2:2], mixed[1:count // 2 * 2:2]
    slack = jnp.minimum(tallies[source_of] - 1, limit - tallies[receiver]) // 2
    slack = jnp.where((source_of == sequence[0]) | (receiver == sequence[0]) | (tallies[receiver] == 0), 0, jnp.maximum(slack, 0))
    moved = jax.random.randint(jax.random.fold_in(own, 4), (count // 2,), 0, 1 << 20) % (slack + 1)
    tallies = tallies.at[source_of].add(-moved).at[receiver].add(moved)
    labels = jnp.searchsorted(jnp.cumsum(tallies), jnp.arange(rows * top), side="right").astype(jnp.int32)
    table = labels.reshape(top, rows).T
    table = table[jax.random.permutation(jax.random.fold_in(own, 1), rows)]
    offset_by = jax.random.randint(jax.random.fold_in(own, 2), (rows, 1), 0, top)
    return jnp.take_along_axis(table, (jnp.arange(top)[None, :] + offset_by) % top, axis=1)


def load_shares(count, total, most, slope, full):
    loads = [(1 << 20) // math.isqrt(rank ** slope) + 1 for rank in range(1, count + 1)]
    largest = most if full else min(most, max(-(-total // count), total * loads[0] // sum(loads)))
    least = 1 if total - largest >= count - 1 else 0
    holding, spare = [largest] + [least] * (count - 1), total - largest - least * (count - 1)
    while spare > 0:
        candidates = [i for i in range(1, count) if holding[i] < largest] or [i for i in range(1, count) if holding[i] < most]
        mass, budget = sum([loads[i] for i in candidates]), spare
        for i in candidates:
            extra = min(most - holding[i], max(1, budget * loads[i] // mass), spare)
            holding[i] = holding[i] + extra
            spare = spare - extra
    return np.array(holding)


def scatter_about(key, dims, deviation, most, cuts=(), held_as=jnp.bfloat16):
    values = deviation * jax.random.normal(key, dims, jnp.float32)
    if cuts:
        values = values * block_levels(key, dims, cuts, -0.22, 0.18)
    return jnp.clip(values, -most, most).astype(held_as)


def setup_inputs(seed: int = 0) -> dict:
    splits = jax.random.split(jax.random.key(seed), 12)
    grad_columns = scatter_about(splits[0], (NF, S * L), 1.0, 6.0, ((0, 128), (1, 4)))
    grad_flux = scatter_about(splits[1], (S, NC), 1.0, 6.0, ((0, 4), (1, 128)), jnp.float32)
    remap_part_keys = jax.random.split(jax.random.fold_in(splits[2], 1), NC // CC)
    remap_part_turns = jax.random.permutation(jax.random.fold_in(splits[2], 3), NC // CC)
    remap_part = jax.vmap(lambda own, number: shared_out(jax.random.fold_in(splits[2], 2), own, number, CC, N_TILE, RB, CAP, 2))(remap_part_keys, remap_part_turns).reshape((NC, RB))
    remap_slot = set_ends(jax.random.randint(splits[3], (NC, RB), 0, CMAX), jax.random.fold_in(splits[3], 1), 0, CMAX - 1).astype(jnp.int32)
    remap_weight = jnp.clip(0.2 + 0.8 * jax.random.uniform(splits[4], (NC, RB), jnp.float32) ** block_levels(splits[4], (NC, RB), ((0, 128),), -0.2, 0.2), 0.2, 1.0)
    col_count = draw_col_count(jax.random.fold_in(splits[11], 71), 0)
    neighbors = draw_neighbors(jax.random.fold_in(splits[11], 71), 0)
    kappa = jnp.clip(jnp.exp(math.log(0.2) - 1.89712 * jax.random.uniform(splits[7], (S,), jnp.float32) ** block_levels(splits[7], (S,), ((0, 4),), -0.2, 0.2)), 0.03, 0.2)
    thickness = jnp.clip(jnp.exp(math.log(2.0) - 2.3025851 * jax.random.uniform(splits[8], (S, L), jnp.float32) ** block_levels(splits[8], (S, L), ((0, 4),), -0.2, 0.2)), 0.2, 2.0)
    vertical = scatter_about(splits[9], (S, L, L), L ** -0.5, 1.0, ((0, 4),))
    reaction = scatter_about(splits[10], (S, S), S ** -0.5, 1.5, ((1, 4),))
    return dict(grad_columns=grad_columns, grad_flux=grad_flux, remap_part=remap_part, remap_slot=remap_slot, remap_weight=remap_weight, col_count=col_count, neighbors=neighbors, kappa=kappa, thickness=thickness, vertical=vertical, reaction=reaction)


def neighbour_targets(neighbors):
    rows = jnp.arange(NF, dtype=jnp.int32)
    part_of = rows // CMAX
    codes = neighbors.astype(jnp.int32)
    excess = codes - CMAX
    own_target = part_of[:, None] * CMAX + codes
    prev_target = (part_of[:, None] - 1) * CMAX + HW + excess
    next_target = (part_of[:, None] + 1) * CMAX + excess - HW
    cross = jnp.where(excess < HW, prev_target, next_target)
    return jnp.where(codes < CMAX, own_target, cross).astype(jnp.int32)


def reference(grad_columns, grad_flux, remap_part, remap_slot, remap_weight, col_count, neighbors, kappa, thickness, vertical, reaction):
    live_mask = (jnp.arange(CMAX)[None, :] < col_count[:, None]).astype(jnp.float32).reshape(NF)
    target = (remap_part * CMAX + remap_slot).reshape(-1).astype(jnp.int32)
    entry_values = (remap_weight[None, :, :] * grad_flux[:, :, None]).reshape(S, NC * RB)
    injected = jnp.zeros((S, NF), jnp.float32).at[:, target].add(entry_values)
    adjoint = live_mask[:, None, None] * (grad_columns.astype(jnp.float32).reshape(NF, S, L) + thickness[None, :, :] * injected.T[:, :, None])
    slots_to = neighbour_targets(neighbors)
    rate = kappa[None, :, None]
    vertical_wide = vertical.astype(jnp.float32)
    for substep in range(SUB):
        spread = rate * adjoint
        bedload = adjoint - NB * rate * adjoint
        for column in range(NB):
            bedload = bedload + jax.ops.segment_sum(spread, slots_to[:, column], num_segments=NF)
        rounded = lax.optimization_barrier(bedload.astype(jnp.bfloat16)).astype(jnp.float32)
        adjoint = jnp.einsum("jsl,slm->jsm", rounded, vertical_wide)
    rounded = lax.optimization_barrier(adjoint.astype(jnp.bfloat16)).astype(jnp.float32)
    mixed = jnp.einsum("jsl,st->jtl", rounded, reaction.astype(jnp.float32))
    grad_state = mixed.reshape(NF, S * L).astype(jnp.bfloat16)
    top_layer = mixed[:, :, 0]
    picked = top_layer[target].reshape(NC, RB, S)
    grad_bottom = jnp.sum(picked * remap_weight[:, :, None], axis=1).T
    return grad_state, grad_bottom
```

```python
import functools

import jax
import jax.numpy as jnp
from jax import lax
from jax.experimental import pallas as pl
from jax.experimental.pallas import tpu as pltpu
from jax.sharding import PartitionSpec as P

SUB = 4
F32 = jnp.float32
BF16 = jnp.bfloat16
MESH = pl.DeviceIdType.MESH
HIGH = lax.Precision.HIGHEST
NT = (((1,), (1,)), ((), ()))
RADIX = 32
PLANES = 6


def dot(a, b):
    return jnp.dot(a, b, preferred_element_type=F32)


def iota(shape, dim):
    return lax.broadcasted_iota(jnp.int32, shape, dim)


def onehot(condition):
    return jnp.where(condition, 1.0, 0.0).astype(BF16)


def dispatch_kernel(tiles, capacity, part_ref, slot_ref, weight_ref, flux_ref, send_ref, rank_ref):
    per_cell, cells = part_ref.shape
    species = flux_ref.shape[0]
    chunk = 256
    before = onehot(iota((chunk, chunk), 0) < iota((chunk, chunk), 1))
    carry = jnp.zeros((tiles, 1), F32)
    total = jnp.zeros((tiles, PLANES * capacity), F32)
    for r in range(per_cell):
        hit = part_ref[r : r + 1, :] == iota((tiles, cells), 0)
        owner = jnp.where(hit, 1.0, 0.0)
        owner_b = owner.astype(BF16)
        for k in range(0, cells, chunk):
            piece = owner[:, k : k + chunk]
            earlier = dot(owner_b[:, k : k + chunk], before) + carry
            rank_ref[r : r + 1, k : k + chunk] = jnp.sum(piece * earlier, axis=0, keepdims=True)
            carry = carry + jnp.sum(piece, axis=1, keepdims=True)
        place = rank_ref[r : r + 1, :].astype(jnp.int32) == iota((capacity, cells), 0)
        slot = slot_ref[r : r + 1, :]
        weight = weight_ref[r : r + 1, :]
        rows = [weight * flux_ref[s : s + 1, :] for s in range(species)]
        rows.append((slot // RADIX).astype(F32))
        rows.append((slot % RADIX).astype(F32))
        wide = jnp.concatenate([jnp.where(place, row, 0.0).astype(BF16) for row in rows], axis=0)
        total = total + lax.dot_general(owner_b, wide, NT, preferred_element_type=F32)
    send_ref[...] = total.astype(BF16)


def column_kernel(
    tiles,
    groups,
    recv_ref,
    columns_ref,
    count_ref,
    neighbors_ref,
    kappa_ref,
    thickness_ref,
    vertical_ref,
    reaction_ref,
    state_ref,
    answer_ref,
    names,
    adjoint,
    operator,
    mixer,
    halo_out,
    halo_in,
    gathered,
    halo_send,
    halo_recv,
    gather_send,
    gather_recv,
):
    slots, width = columns_ref.shape
    species, layers = thickness_ref.shape
    rim = slots // 8
    nbr_count = neighbors_ref.shape[0]
    entries = recv_ref.shape[1]
    tile, spec = lax.axis_index("tile"), lax.axis_index("spec")
    following = lax.rem(tile + 1, tiles)
    previous = lax.rem(tile + tiles - 1, tiles)
    peers = [lax.rem(spec + d, groups) for d in range(1, groups)]

    barrier = pltpu.get_barrier_semaphore()
    for other in (previous, following):
        pl.semaphore_signal(barrier, inc=1, device_id=(other, spec), device_id_type=MESH)
    for other in peers:
        pl.semaphore_signal(barrier, inc=1, device_id=(tile, other), device_id_type=MESH)

    step = 256
    for m in range(0, slots + 2 * rim, step):
        code = iota((step, slots), 0) + m
        count = jnp.zeros((step, slots), F32)
        for n in range(nbr_count):
            count = count + jnp.where(neighbors_ref[n : n + 1, :] == code, 1.0, 0.0)
        names[m : m + step, :] = count.astype(BF16)

    lane = iota((1, width), 1)
    layer_to_lane = onehot(iota((layers, width), 0) == iota((layers, width), 1) % layers)
    same_species = iota((width, width), 0) // layers == iota((width, width), 1) // layers
    operator[...] = jnp.where(same_species, dot(vertical_ref[...], layer_to_lane), 0.0).astype(BF16)
    all_species = groups * species
    wide = groups * width
    row_species = onehot(iota((wide, all_species), 0) // layers == iota((wide, all_species), 1))
    lane_species = onehot(iota((species, width), 0) == iota((species, width), 1) // layers)
    by_row = dot(row_species, reaction_ref[...]).astype(BF16)
    spread_out = dot(by_row, lane_species)
    same_layer = iota((wide, width), 0) % layers == iota((wide, width), 1) % layers
    mixer[...] = jnp.where(same_layer, spread_out, 0.0).astype(BF16)
    rate = jnp.zeros((1, width), F32)
    for s in range(species):
        rate = rate + jnp.where(lane // layers == s, kappa_ref[0:1, s : s + 1], 0.0)
    thick_rows = jnp.dot(
        thickness_ref[...], layer_to_lane.astype(F32), precision=HIGH, preferred_element_type=F32
    )
    thick = jnp.zeros((1, width), F32)
    for s in range(species):
        thick = thick + jnp.where(lane // layers == s, thick_rows[s : s + 1, :], 0.0)

    block = 1024
    digits = slots // RADIX
    injected = jnp.zeros((digits, species * RADIX), F32)
    for e in range(0, entries, block):
        high = recv_ref[species : species + 1, e : e + block].astype(jnp.int32)
        low = recv_ref[species + 1 : species + 2, e : e + block].astype(jnp.int32)
        high_hot = onehot(high == iota((digits, block), 0))
        low_hit = low == iota((RADIX, block), 0)
        values = [
            jnp.where(low_hit, recv_ref[s : s + 1, e : e + block], 0.0).astype(BF16)
            for s in range(species)
        ]
        injected = injected + lax.dot_general(
            high_hot, jnp.concatenate(values, axis=0), NT, preferred_element_type=F32
        )
    slot_digit = onehot(iota((slots, digits), 0) // RADIX == iota((slots, digits), 1))
    own_low = iota((slots, width), 0) % RADIX == iota((slots, width), 1) % RADIX
    block_ones = onehot(same_species)
    upper = injected.astype(BF16)
    lower = (injected - upper.astype(F32)).astype(BF16)
    added = jnp.zeros((slots, width), F32)
    for part in (upper, lower):
        chosen = jnp.where(own_low, dot(slot_digit, part), 0.0).astype(BF16)
        added = added + dot(chosen, block_ones)
    live = iota((slots, 1), 0) < count_ref[0, 0]
    adjoint[...] = jnp.where(live, columns_ref[...].astype(F32) + thick * added, 0.0)

    pl.semaphore_wait(barrier, groups + 1)

    keep = 1.0 - nbr_count * rate
    for substep in range(SUB):
        spread = (rate * adjoint[...]).astype(BF16)
        outer = dot(names[slots : slots + 2 * rim, :], spread)
        halo_out[substep] = outer.astype(BF16)
        copies = []
        for side, other in enumerate((previous, following)):
            copy = pltpu.make_async_remote_copy(
                src_ref=halo_out.at[substep, pl.ds(side * rim, rim)],
                dst_ref=halo_in.at[substep, pl.ds((1 - side) * rim, rim)],
                send_sem=halo_send.at[substep, side],
                recv_sem=halo_recv.at[substep, side],
                device_id=(other, spec),
                device_id_type=MESH,
            )
            copy.start()
            copies.append(copy)
        inner = dot(names[0:slots, :], spread)
        bedload = keep * adjoint[...] + inner
        rest = bedload[2 * rim :, :].astype(BF16)
        rest = dot(rest, operator[...])
        for copy in copies:
            copy.wait()
        front = bedload[: 2 * rim, :] + halo_in[substep].astype(F32)
        front = dot(front.astype(BF16), operator[...])
        if substep < SUB - 1:
            adjoint[0 : 2 * rim, :] = front
            adjoint[2 * rim :, :] = rest
        else:
            gathered[spec, 0 : 2 * rim, :] = front.astype(BF16)
            gathered[spec, 2 * rim :, :] = rest.astype(BF16)

    copies = []
    for d, other in enumerate(peers):
        copy = pltpu.make_async_remote_copy(
            src_ref=gathered.at[spec],
            dst_ref=gathered.at[spec],
            send_sem=gather_send.at[d],
            recv_sem=gather_recv.at[d],
            device_id=(tile, other),
            device_id_type=MESH,
        )
        copy.start()
        copies.append(copy)
    mine = gathered[spec]
    mixed = dot(mine, mixer[pl.ds(pl.multiple_of(spec * width, width), width), :])
    for copy in copies:
        copy.wait()
    for d in range(1, groups):
        origin = lax.rem(spec + groups - d, groups)
        mixed = mixed + dot(
            gathered[origin], mixer[pl.ds(pl.multiple_of(origin * width, width), width), :]
        )
    state = mixed.astype(BF16)
    state_ref[...] = state

    top_to_low = onehot(same_species & (iota((width, width), 0) % layers == 0))
    spread_top = jnp.where(own_low, dot(state, top_to_low), 0.0).astype(BF16)
    digit_slot = onehot(iota((digits, slots), 0) == iota((digits, slots), 1) // RADIX)
    table = dot(digit_slot, spread_top).T.astype(BF16)
    for e in range(0, entries, block):
        high = recv_ref[species : species + 1, e : e + block].astype(jnp.int32)
        low = recv_ref[species + 1 : species + 2, e : e + block].astype(jnp.int32)
        high_hot = onehot(high == iota((digits, block), 0))
        low_hit = low == iota((RADIX, block), 0)
        found = dot(table, high_hot)
        for s in range(species):
            answer_ref[s : s + 1, e : e + block] = jnp.sum(
                jnp.where(low_hit, found[s * RADIX : (s + 1) * RADIX, :], 0.0), axis=0, keepdims=True
            )


def combine_kernel(capacity, returned_ref, part_ref, rank_ref, weight_ref, bottom_ref):
    per_cell, cells = part_ref.shape
    species = bottom_ref.shape[0]
    tiles = returned_ref.shape[1]
    totals = [jnp.zeros((1, cells), F32) for _ in range(species)]
    for r in range(per_cell):
        owner = onehot(part_ref[r : r + 1, :] == iota((tiles, cells), 0))
        place = rank_ref[r : r + 1, :].astype(jnp.int32) == iota((capacity, cells), 0)
        found = dot(returned_ref[...], owner)
        for s in range(species):
            picked = jnp.sum(
                jnp.where(place, found[s * capacity : (s + 1) * capacity, :], 0.0),
                axis=0,
                keepdims=True,
            )
            totals[s] = totals[s] + weight_ref[r : r + 1, :] * picked
    for s in range(species):
        bottom_ref[s : s + 1, :] = totals[s]


def whole():
    return pl.BlockSpec(memory_space=pltpu.VMEM)


def body(
    grad_columns,
    grad_flux,
    remap_part,
    remap_slot,
    remap_weight,
    col_count,
    neighbors,
    kappa,
    thickness,
    vertical,
    reaction,
):
    tiles, groups = lax.axis_size("tile"), lax.axis_size("spec")
    slots, width = grad_columns.shape
    species, layers = thickness.shape
    cells, per_cell = remap_part.shape
    capacity = 2 * cells * per_cell // tiles
    rim = slots // 8
    part_t, slot_t, weight_t = remap_part.T, remap_slot.T, remap_weight.T
    send, rank = pl.pallas_call(
        functools.partial(dispatch_kernel, tiles, capacity),
        out_shape=(
            jax.ShapeDtypeStruct((tiles, PLANES * capacity), BF16),
            jax.ShapeDtypeStruct((per_cell, cells), F32),
        ),
        in_specs=[whole()] * 4,
        out_specs=(whole(), whole()),
        compiler_params=pltpu.CompilerParams(vmem_limit_bytes=40 * 2**20),
        name="dispatch",
    )(part_t, slot_t, weight_t, grad_flux)
    recv = lax.all_to_all(send, "tile", split_axis=0, concat_axis=0, tiled=True)
    recv = recv.reshape(tiles, PLANES, capacity).transpose(1, 0, 2)
    recv = recv.reshape(PLANES, tiles * capacity).astype(F32)
    entries = tiles * capacity
    grad_state, answer = pl.pallas_call(
        functools.partial(column_kernel, tiles, groups),
        out_shape=(
            jax.ShapeDtypeStruct((slots, width), BF16),
            jax.ShapeDtypeStruct((species, entries), F32),
        ),
        in_specs=[whole(), whole(), pl.BlockSpec(memory_space=pltpu.SMEM)] + [whole()] * 5,
        out_specs=(whole(), whole()),
        scratch_shapes=[
            pltpu.VMEM((slots + 2 * rim, slots), BF16),
            pltpu.VMEM((slots, width), F32),
            pltpu.VMEM((width, width), BF16),
            pltpu.VMEM((groups * width, width), BF16),
            pltpu.VMEM((SUB, 2 * rim, width), BF16),
            pltpu.VMEM((SUB, 2 * rim, width), BF16),
            pltpu.VMEM((groups, slots, width), BF16),
            pltpu.SemaphoreType.DMA((SUB, 2)),
            pltpu.SemaphoreType.DMA((SUB, 2)),
            pltpu.SemaphoreType.DMA((groups - 1,)),
            pltpu.SemaphoreType.DMA((groups - 1,)),
        ],
        compiler_params=pltpu.CompilerParams(
            collective_id=0, has_side_effects=True, vmem_limit_bytes=48 * 2**20
        ),
        name="columns",
    )(
        recv,
        grad_columns,
        col_count.reshape(1, 1),
        neighbors.T,
        kappa.reshape(1, species),
        thickness,
        vertical.reshape(width, layers),
        reaction,
    )
    answer = answer.astype(BF16).reshape(species, tiles, capacity).transpose(1, 0, 2)
    answer = answer.reshape(tiles, species * capacity)
    returned = lax.all_to_all(answer, "tile", split_axis=0, concat_axis=0, tiled=True)
    grad_bottom = pl.pallas_call(
        functools.partial(combine_kernel, capacity),
        out_shape=jax.ShapeDtypeStruct((species, cells), F32),
        in_specs=[whole()] * 4,
        out_specs=whole(),
        compiler_params=pltpu.CompilerParams(vmem_limit_bytes=40 * 2**20),
        name="combine",
    )(returned.T, part_t, rank, weight_t)
    return (grad_state, grad_bottom)


def solution(mesh):
    placed = (
        P("tile", "spec"),
        P("spec", "tile"),
        P("tile", None),
        P("tile", None),
        P("tile", None),
        P("tile"),
        P("tile", None),
        P("spec"),
        P("spec", None),
        P("spec", None, None),
        P(None, "spec"),
    )
    return jax.shard_map(
        body,
        mesh=mesh,
        in_specs=placed,
        out_specs=(P("tile", "spec"), P("spec", "tile")),
        check_vma=False,
    )
```

```python
import functools

import jax
import jax.numpy as jnp
from jax import lax
from jax.experimental import pallas as pl
from jax.experimental.pallas import tpu as pltpu
from jax.sharding import PartitionSpec as P

SUB = 4
F32 = jnp.float32
BF16 = jnp.bfloat16
MESH = pl.DeviceIdType.MESH
HIGH = lax.Precision.HIGHEST
NT = (((1,), (1,)), ((), ()))
RADIX = 32
ROW = 16


def dot(a, b):
    return jnp.dot(a, b, preferred_element_type=F32)


def iota(shape, dim):
    return lax.broadcasted_iota(jnp.int32, shape, dim)


def onehot(condition):
    return jnp.where(condition, 1.0, 0.0).astype(BF16)


def exchange(tile, spec, outer, source, stage, target, sems, between):
    mine, row = lax.rem(tile, ROW), tile // ROW
    first_send, first_recv, second_send, second_recv, local = sems
    keep = pltpu.make_async_copy(source.at[:, mine], stage.at[:, mine], local.at[0])
    keep.start()
    copies = []
    for d in range(1, ROW):
        other = lax.rem(mine + d, ROW)
        copy = pltpu.make_async_remote_copy(
            src_ref=source.at[:, other],
            dst_ref=stage.at[:, mine],
            send_sem=first_send.at[d - 1],
            recv_sem=first_recv.at[d - 1],
            device_id=(row * ROW + other, spec),
            device_id_type=MESH,
        )
        copy.start()
        copies.append(copy)
    between[0]()
    keep.wait()
    for copy in copies:
        copy.wait()
    keep = pltpu.make_async_copy(stage.at[row], target.at[row], local.at[1])
    keep.start()
    copies = []
    for d in range(1, outer):
        other = lax.rem(row + d, outer)
        copy = pltpu.make_async_remote_copy(
            src_ref=stage.at[other],
            dst_ref=target.at[row],
            send_sem=second_send.at[d - 1],
            recv_sem=second_recv.at[d - 1],
            device_id=(other * ROW + mine, spec),
            device_id_type=MESH,
        )
        copy.start()
        copies.append(copy)
    between[1]()
    keep.wait()
    for copy in copies:
        copy.wait()


def step_kernel(
    tiles,
    groups,
    part_hbm,
    slot_hbm,
    weight_hbm,
    flux_hbm,
    columns_hbm,
    neighbors_hbm,
    vertical_hbm,
    thickness_ref,
    count_ref,
    kappa_ref,
    reaction_ref,
    state_ref,
    bottom_ref,
    part_ref,
    slot_ref,
    weight_ref,
    flux_ref,
    columns_ref,
    neighbors_ref,
    vertical_ref,
    rank_ref,
    packed,
    names,
    adjoint,
    operator,
    mixer,
    send,
    stage,
    recv,
    answer,
    back,
    returned,
    halo_out,
    halo_in,
    gathered,
    tables,
    load_sem,
    halo_send,
    halo_recv,
    gather_send,
    gather_recv,
    table_send,
    table_recv,
    *sems,
):
    slots, width = columns_ref.shape
    species, layers = thickness_ref.shape
    per_cell, cells = part_ref.shape
    outer = tiles // ROW
    half = width // 2
    rim = slots // 8
    nbr_count = neighbors_ref.shape[0]
    tile, spec = lax.axis_index("tile"), lax.axis_index("spec")
    mine, row = lax.rem(tile, ROW), tile // ROW
    following = lax.rem(tile + 1, tiles)
    previous = lax.rem(tile + tiles - 1, tiles)
    peers = [lax.rem(spec + d, groups) for d in range(1, groups)]

    loads = []
    for k, (src, dst) in enumerate(
        (
            (part_hbm, part_ref),
            (slot_hbm, slot_ref),
            (weight_hbm, weight_ref),
            (flux_hbm, flux_ref),
            (neighbors_hbm, neighbors_ref),
            (columns_hbm, columns_ref),
            (vertical_hbm, vertical_ref),
        )
    ):
        load = pltpu.make_async_copy(src, dst, load_sem.at[k])
        load.start()
        loads.append(load)

    barrier = pltpu.get_barrier_semaphore()
    partners = [(other, spec) for other in (previous, following)]
    partners += [(tile, other) for other in peers]
    partners += [(row * ROW + lax.rem(mine + d, ROW), spec) for d in range(1, ROW)]
    partners += [(lax.rem(row + d, outer) * ROW + mine, spec) for d in range(1, outer)]
    for partner in partners:
        pl.semaphore_signal(barrier, inc=1, device_id=partner, device_id_type=MESH)

    for load in loads[:4]:
        load.wait()
    chunk = 256
    before = onehot(iota((chunk, chunk), 0) < iota((chunk, chunk), 1))
    carry = jnp.zeros((tiles, 1), F32)
    total = jnp.zeros((tiles, 4 * width), F32)
    for r in range(per_cell):
        hit = part_ref[r : r + 1, :] == iota((tiles, cells), 0)
        owner = jnp.where(hit, 1.0, 0.0)
        owner_b = owner.astype(BF16)
        for k in range(0, cells, chunk):
            piece = owner[:, k : k + chunk]
            earlier = dot(owner_b[:, k : k + chunk], before) + carry
            rank_ref[r : r + 1, k : k + chunk] = jnp.sum(piece * earlier, axis=0, keepdims=True)
            carry = carry + jnp.sum(piece, axis=1, keepdims=True)
        place = rank_ref[r : r + 1, :].astype(jnp.int32) == iota((half, cells), 0)
        slot = slot_ref[r : r + 1, :]
        weight = weight_ref[r : r + 1, :]
        rows = [weight * flux_ref[s : s + 1, :] for s in range(species)]
        rows.append((slot // RADIX).astype(F32))
        rows.append((slot % RADIX).astype(F32))
        pieces = [jnp.where(place, value, 0.0).astype(BF16) for value in rows]
        pieces = pieces[:5] + pieces[4:] + pieces[5:]
        wide = jnp.concatenate(pieces, axis=0)
        total = total + lax.dot_general(owner_b, wide, NT, preferred_element_type=F32)
    for k in range(4):
        packed[pl.ds(k, tiles, stride=4), :] = total[:, k * width : (k + 1) * width]
    for d in range(tiles):
        send[d // ROW, d % ROW] = packed[4 * d : 4 * d + 4, :].astype(BF16)

    step = 256

    def name(m):
        code = iota((step, slots), 0) + m
        count = jnp.zeros((step, slots), F32)
        for n in range(nbr_count):
            count = count + jnp.where(neighbors_ref[n : n + 1, :] == code, 1.0, 0.0)
        names[m : m + step, :] = count.astype(BF16)

    def under_first():
        loads[4].wait()
        for m in range(0, 3 * step, step):
            name(m)

    same_species = iota((width, width), 0) // layers == iota((width, width), 1) // layers

    def under_second():
        for m in range(3 * step, slots + 2 * rim, step):
            name(m)
        layer_to_lane = onehot(iota((layers, width), 0) == iota((layers, width), 1) % layers)
        for load in loads[5:]:
            load.wait()
        tall = dot(vertical_ref[...], layer_to_lane)
        operator[...] = jnp.where(same_species, tall, 0.0).astype(BF16)
        all_species = groups * species
        wide = groups * width
        row_species = onehot(iota((wide, all_species), 0) // layers == iota((wide, all_species), 1))
        lane_species = onehot(iota((species, width), 0) == iota((species, width), 1) // layers)
        by_row = lax.dot_general(row_species, reaction_ref[...], NT, preferred_element_type=F32)
        spread_out = dot(by_row.astype(BF16), lane_species)
        same_layer = iota((wide, width), 0) % layers == iota((wide, width), 1) % layers
        mixer[...] = jnp.where(same_layer, spread_out, 0.0).astype(BF16)

    pl.semaphore_wait(barrier, len(partners))
    exchange(
        tile, spec, outer, send, stage, recv, [s.at[0] for s in sems], (under_first, under_second)
    )

    lane = iota((1, width), 1)
    left = lane < half
    rate = jnp.zeros((1, width), F32)
    for s in range(species):
        rate = rate + jnp.where(lane // layers == s, kappa_ref[0:1, s : s + 1], 0.0)
    thick_rows = jnp.dot(
        thickness_ref[...],
        jnp.where(iota((layers, width), 0) == iota((layers, width), 1) % layers, 1.0, 0.0),
        precision=HIGH,
        preferred_element_type=F32,
    )
    thick = jnp.zeros((1, width), F32)
    for s in range(species):
        thick = thick + jnp.where(lane // layers == s, thick_rows[s : s + 1, :], 0.0)

    digits = slots // RADIX
    digit = iota((digits, width), 0)

    def inject(o, injected):
        highs, wides = [], []
        for i in range(ROW):
            x = recv[o, i].astype(F32)
            highs.append(onehot(x[2:3, :].astype(jnp.int32) == digit))
            low_hit = x[3:4, :].astype(jnp.int32) == digit
            values = []
            for s in range(species):
                value = jnp.where(left if s % 2 == 0 else ~left, x[s // 2 : s // 2 + 1, :], 0.0)
                values.append(jnp.where(low_hit, value, 0.0).astype(BF16))
            wides.append(jnp.concatenate(values, axis=0))
        return injected + lax.dot_general(
            jnp.concatenate(highs, axis=1),
            jnp.concatenate(wides, axis=1),
            NT,
            preferred_element_type=F32,
        )

    injected = lax.fori_loop(0, outer, inject, jnp.zeros((digits, width), F32))
    slot_digit = onehot(iota((slots, digits), 0) // RADIX == iota((slots, digits), 1))
    own_low = iota((slots, width), 0) % RADIX == iota((slots, width), 1) % RADIX
    block_ones = onehot(same_species)
    upper = injected.astype(BF16)
    lower = (injected - upper.astype(F32)).astype(BF16)
    added = jnp.zeros((slots, width), F32)
    for part in (upper, lower):
        chosen = jnp.where(own_low, dot(slot_digit, part), 0.0).astype(BF16)
        added = added + dot(chosen, block_ones)
    live = iota((slots, 1), 0) < count_ref[0, 0]
    adjoint[...] = jnp.where(live, columns_ref[...].astype(F32) + thick * added, 0.0)

    keep = 1.0 - nbr_count * rate
    for substep in range(SUB):
        spread = (rate * adjoint[...]).astype(BF16)
        outside = dot(names[slots : slots + 2 * rim, :], spread)
        halo_out[substep] = outside.astype(BF16)
        copies = []
        for side, other in enumerate((previous, following)):
            copy = pltpu.make_async_remote_copy(
                src_ref=halo_out.at[substep, pl.ds(side * rim, rim)],
                dst_ref=halo_in.at[substep, pl.ds((1 - side) * rim, rim)],
                send_sem=halo_send.at[substep, side],
                recv_sem=halo_recv.at[substep, side],
                device_id=(other, spec),
                device_id_type=MESH,
            )
            copy.start()
            copies.append(copy)
        inner = dot(names[0:slots, :], spread)
        bedload = keep * adjoint[...] + inner
        rest = bedload[2 * rim :, :].astype(BF16)
        rest = dot(rest, operator[...])
        for copy in copies:
            copy.wait()
        front = bedload[: 2 * rim, :] + halo_in[substep].astype(F32)
        front = dot(front.astype(BF16), operator[...])
        if substep < SUB - 1:
            adjoint[0 : 2 * rim, :] = front
            adjoint[2 * rim :, :] = rest
        else:
            gathered[spec, 0 : 2 * rim, :] = front.astype(BF16)
            gathered[spec, 2 * rim :, :] = rest.astype(BF16)

    own = gathered[spec]
    top_to_low = onehot(same_species & (iota((width, width), 0) % layers == 0))
    spread_top = jnp.where(own_low, dot(own, top_to_low), 0.0).astype(BF16)
    digit_slot = onehot(iota((digits, slots), 0) == iota((digits, slots), 1) // RADIX)
    tables[spec] = dot(digit_slot, spread_top).astype(BF16)

    def share(buffer, send_sem, recv_sem):
        copies = []
        for d, other in enumerate(peers):
            copy = pltpu.make_async_remote_copy(
                src_ref=buffer.at[spec],
                dst_ref=buffer.at[spec],
                send_sem=send_sem.at[d],
                recv_sem=recv_sem.at[d],
                device_id=(tile, other),
                device_id_type=MESH,
            )
            copy.start()
            copies.append(copy)
        return copies

    table_copies = share(tables, table_send, table_recv)
    gather_copies = share(gathered, gather_send, gather_recv)

    def mixer_of(origin):
        return mixer[pl.ds(pl.multiple_of(origin * width, width), width), :]

    for copy in table_copies:
        copy.wait()
    table = jnp.zeros((digits, width), F32)
    for g in range(groups):
        table = table + dot(tables[g], mixer[g * width : (g + 1) * width, :])
    table = table.T.astype(BF16)

    def reply(o, carried):
        highs, hits = [], []
        for i in range(ROW):
            x = recv[o, i].astype(F32)
            highs.append(onehot(x[2:3, :].astype(jnp.int32) == digit))
            hits.append(x[3:4, :].astype(jnp.int32) == digit)
        found = dot(table, jnp.concatenate(highs, axis=1))
        for i in range(ROW):
            lines = []
            for k in range(species // 2):
                even, odd = [
                    found[s * RADIX : (s + 1) * RADIX, i * width : (i + 1) * width]
                    for s in (2 * k, 2 * k + 1)
                ]
                picked = jnp.where(hits[i], jnp.where(left, even, odd), 0.0)
                lines.append(jnp.sum(picked, axis=0, keepdims=True))
            answer[o, i] = jnp.concatenate(lines, axis=0).astype(BF16)
        return carried

    lax.fori_loop(0, outer, reply, 0)

    def under_reply():
        pass

    def under_return():
        mixed = dot(own, mixer_of(spec))
        for copy in gather_copies:
            copy.wait()
        for d in range(1, groups):
            origin = lax.rem(spec + groups - d, groups)
            mixed = mixed + dot(gathered[origin], mixer_of(origin))
        state_ref[...] = mixed.astype(BF16)

    exchange(
        tile,
        spec,
        outer,
        answer,
        back,
        returned,
        [s.at[1] for s in sems],
        (under_reply, under_return),
    )
    for p in range(tiles):
        packed[2 * p : 2 * p + 2, :] = returned[p // ROW, p % ROW].astype(F32)
    by_place = jnp.concatenate(
        [packed[pl.ds(k, tiles, stride=2), :].T for k in range(species // 2)], axis=0
    ).astype(BF16)
    totals = [jnp.zeros((1, cells), F32) for _ in range(species)]
    for r in range(per_cell):
        owner = onehot(part_ref[r : r + 1, :] == iota((tiles, cells), 0))
        place = rank_ref[r : r + 1, :].astype(jnp.int32) == iota((half, cells), 0)
        found = dot(by_place, owner)
        for s in range(species):
            picked = jnp.where(place, found[s * half : (s + 1) * half, :], 0.0)
            picked = jnp.sum(picked, axis=0, keepdims=True)
            totals[s] = totals[s] + weight_ref[r : r + 1, :] * picked
    for s in range(species):
        bottom_ref[s : s + 1, :] = totals[s]


def whole():
    return pl.BlockSpec(memory_space=pltpu.VMEM)


def body(
    grad_columns,
    grad_flux,
    remap_part,
    remap_slot,
    remap_weight,
    col_count,
    neighbors,
    kappa,
    thickness,
    vertical,
    reaction,
):
    tiles, groups = lax.axis_size("tile"), lax.axis_size("spec")
    slots, width = grad_columns.shape
    species, layers = thickness.shape
    cells, per_cell = remap_part.shape
    rim = slots // 8
    outer = tiles // ROW
    digits = slots // RADIX
    nbr_count = neighbors.shape[1]
    dma = pltpu.SemaphoreType.DMA
    vmem = pltpu.VMEM
    grad_state, grad_bottom = pl.pallas_call(
        functools.partial(step_kernel, tiles, groups),
        out_shape=(
            jax.ShapeDtypeStruct((slots, width), BF16),
            jax.ShapeDtypeStruct((species, cells), F32),
        ),
        in_specs=[pl.BlockSpec(memory_space=pl.ANY)] * 7
        + [whole(), pl.BlockSpec(memory_space=pltpu.SMEM), whole(), whole()],
        out_specs=(whole(), whole()),
        scratch_shapes=[
            vmem((per_cell, cells), jnp.int32),
            vmem((per_cell, cells), jnp.int32),
            vmem((per_cell, cells), F32),
            vmem((species, cells), F32),
            vmem((slots, width), BF16),
            vmem((nbr_count, slots), jnp.int32),
            vmem((width, layers), BF16),
            vmem((per_cell, cells), F32),
            vmem((4 * tiles, width), F32),
            vmem((slots + 2 * rim, slots), BF16),
            vmem((slots, width), F32),
            vmem((width, width), BF16),
            vmem((groups * width, width), BF16),
            vmem((outer, ROW, 4, width), BF16),
            vmem((outer, ROW, 4, width), BF16),
            vmem((outer, ROW, 4, width), BF16),
            vmem((outer, ROW, 2, width), BF16),
            vmem((outer, ROW, 2, width), BF16),
            vmem((outer, ROW, 2, width), BF16),
            vmem((SUB, 2 * rim, width), BF16),
            vmem((SUB, 2 * rim, width), BF16),
            vmem((groups, slots, width), BF16),
            vmem((groups, digits, width), BF16),
            dma((7,)),
            dma((SUB, 2)),
            dma((SUB, 2)),
            dma((groups - 1,)),
            dma((groups - 1,)),
            dma((groups - 1,)),
            dma((groups - 1,)),
            dma((2, ROW - 1)),
            dma((2, ROW - 1)),
            dma((2, outer - 1)),
            dma((2, outer - 1)),
            dma((2, 2)),
        ],
        compiler_params=pltpu.CompilerParams(
            collective_id=0, has_side_effects=True, vmem_limit_bytes=56 * 2**20
        ),
        name="step",
    )(
        remap_part.T,
        remap_slot.T,
        remap_weight.T,
        grad_flux,
        grad_columns,
        neighbors.T,
        vertical.reshape(width, layers),
        thickness,
        col_count.reshape(1, 1),
        kappa.reshape(1, species),
        reaction.T,
    )
    return (grad_state, grad_bottom)


def solution(mesh):
    placed = (
        P("tile", "spec"),
        P("spec", "tile"),
        P("tile", None),
        P("tile", None),
        P("tile", None),
        P("tile"),
        P("tile", None),
        P("spec"),
        P("spec", None),
        P("spec", None, None),
        P(None, "spec"),
    )
    return jax.shard_map(
        body,
        mesh=mesh,
        in_specs=placed,
        out_specs=(P("tile", "spec"), P("spec", "tile")),
        check_vma=False,
    )
```

```python
import functools

import jax
import jax.numpy as jnp
from jax import lax
from jax.experimental import pallas as pl
from jax.experimental.pallas import tpu as pltpu
from jax.sharding import PartitionSpec as P

SUB = 4
F32 = jnp.float32
BF16 = jnp.bfloat16
MESH = pl.DeviceIdType.MESH
HIGH = lax.Precision.HIGHEST
NT = (((1,), (1,)), ((), ()))
RADIX = 32
ROW = 16


def dot(a, b):
    return jnp.dot(a, b, preferred_element_type=F32)


def iota(shape, dim):
    return lax.broadcasted_iota(jnp.int32, shape, dim)


def onehot(condition):
    return jnp.where(condition, 1.0, 0.0).astype(BF16)


def exchange(tile, spec, outer, source, stage, target, sems, between):
    mine, row = lax.rem(tile, ROW), tile // ROW
    first_send, first_recv, second_send, second_recv, local = sems
    keep = pltpu.make_async_copy(source.at[:, mine], stage.at[:, mine], local.at[0])
    keep.start()
    copies = []
    for d in range(1, ROW):
        other = lax.rem(mine + d, ROW)
        copy = pltpu.make_async_remote_copy(
            src_ref=source.at[:, other],
            dst_ref=stage.at[:, mine],
            send_sem=first_send.at[d - 1],
            recv_sem=first_recv.at[d - 1],
            device_id=(row * ROW + other, spec),
            device_id_type=MESH,
        )
        copy.start()
        copies.append(copy)
    between[0]()
    keep.wait()
    for copy in copies:
        copy.wait()
    keep = pltpu.make_async_copy(stage.at[row], target.at[row], local.at[1])
    keep.start()
    copies = []
    for d in range(1, outer):
        other = lax.rem(row + d, outer)
        copy = pltpu.make_async_remote_copy(
            src_ref=stage.at[other],
            dst_ref=target.at[row],
            send_sem=second_send.at[d - 1],
            recv_sem=second_recv.at[d - 1],
            device_id=(other * ROW + mine, spec),
            device_id_type=MESH,
        )
        copy.start()
        copies.append(copy)
    between[1]()
    keep.wait()
    for copy in copies:
        copy.wait()


def step_kernel(
    tiles,
    groups,
    part_hbm,
    slot_hbm,
    weight_hbm,
    flux_hbm,
    columns_hbm,
    neighbors_hbm,
    vertical_hbm,
    thickness_hbm,
    count_hbm,
    kappa_hbm,
    reaction_hbm,
    state_ref,
    bottom_ref,
    part_ref,
    slot_ref,
    weight_ref,
    flux_ref,
    columns_ref,
    neighbors_ref,
    vertical_ref,
    thickness_ref,
    count_ref,
    kappa_ref,
    reaction_ref,
    rank_ref,
    packed,
    names,
    adjoint,
    operator,
    mixer,
    send,
    stage,
    recv,
    answer,
    back,
    returned,
    halo_out,
    halo_in,
    gathered,
    tables,
    digit_hot,
    rims,
    beyond,
    load_sem,
    halo_send,
    halo_recv,
    gather_send,
    gather_recv,
    table_send,
    table_recv,
    *sems,
):
    slots, width = columns_ref.shape
    species, layers = thickness_ref.shape
    per_cell, cells = part_ref.shape
    outer = tiles // ROW
    half = width // 2
    rim = slots // 8
    nbr_count = neighbors_ref.shape[0]
    tile, spec = lax.axis_index("tile"), lax.axis_index("spec")
    mine, row = lax.rem(tile, ROW), tile // ROW
    following = lax.rem(tile + 1, tiles)
    previous = lax.rem(tile + tiles - 1, tiles)
    peers = [lax.rem(spec + d, groups) for d in range(1, groups)]

    loads = []
    for k, (src, dst) in enumerate(
        (
            (part_hbm, part_ref),
            (slot_hbm, slot_ref),
            (weight_hbm, weight_ref),
            (flux_hbm, flux_ref),
            (neighbors_hbm, neighbors_ref),
            (columns_hbm, columns_ref),
            (vertical_hbm, vertical_ref),
            (thickness_hbm, thickness_ref),
            (count_hbm, count_ref),
            (kappa_hbm, kappa_ref),
            (reaction_hbm, reaction_ref),
        )
    ):
        load = pltpu.make_async_copy(src, dst, load_sem.at[k])
        load.start()
        loads.append(load)

    barrier = pltpu.get_barrier_semaphore()
    partners = [(other, spec) for other in (previous, following)]
    partners += [(tile, other) for other in peers]
    partners += [(row * ROW + lax.rem(mine + d, ROW), spec) for d in range(1, ROW)]
    partners += [(lax.rem(row + d, outer) * ROW + mine, spec) for d in range(1, outer)]
    for partner in partners:
        pl.semaphore_signal(barrier, inc=1, device_id=partner, device_id_type=MESH)

    for load in loads[:4]:
        load.wait()
    chunk = 256
    before = onehot(iota((chunk, chunk), 0) < iota((chunk, chunk), 1))
    carry = jnp.zeros((tiles, 1), F32)
    total = jnp.zeros((tiles, 4 * width), F32)
    for r in range(per_cell):
        hit = part_ref[r : r + 1, :] == iota((tiles, cells), 0)
        owner = jnp.where(hit, 1.0, 0.0)
        owner_b = owner.astype(BF16)
        for k in range(0, cells, chunk):
            piece = owner[:, k : k + chunk]
            earlier = dot(owner_b[:, k : k + chunk], before) + carry
            rank_ref[r : r + 1, k : k + chunk] = jnp.sum(piece * earlier, axis=0, keepdims=True)
            carry = carry + jnp.sum(piece, axis=1, keepdims=True)
        place = rank_ref[r : r + 1, :].astype(jnp.int32) == iota((half, cells), 0)
        slot = slot_ref[r : r + 1, :]
        weight = weight_ref[r : r + 1, :]
        rows = [weight * flux_ref[s : s + 1, :] for s in range(species)]
        rows.append((slot // RADIX).astype(F32))
        rows.append((slot % RADIX).astype(F32))
        pieces = [jnp.where(place, value, 0.0).astype(BF16) for value in rows]
        pieces = pieces[:5] + pieces[4:] + pieces[5:]
        wide = jnp.concatenate(pieces, axis=0)
        total = total + lax.dot_general(owner_b, wide, NT, preferred_element_type=F32)
    for k in range(4):
        packed[pl.ds(k, tiles, stride=4), :] = total[:, k * width : (k + 1) * width]
    for d in range(tiles):
        send[d // ROW, d % ROW] = packed[4 * d : 4 * d + 4, :].astype(BF16)

    step = 256

    def name(m):
        code = iota((step, slots), 0) + m
        count = jnp.zeros((step, slots), F32)
        for n in range(nbr_count):
            count = count + jnp.where(neighbors_ref[n : n + 1, :] == code, 1.0, 0.0)
        names[m : m + step, :] = count.astype(BF16)

    def under_first():
        loads[4].wait()
        for m in range(0, 3 * step, step):
            name(m)

    same_species = iota((width, width), 0) // layers == iota((width, width), 1) // layers

    def under_second():
        for m in range(3 * step, slots + 2 * rim, step):
            name(m)
        layer_to_lane = onehot(iota((layers, width), 0) == iota((layers, width), 1) % layers)
        for load in loads[5:]:
            load.wait()
        tall = dot(vertical_ref[...], layer_to_lane)
        operator[...] = jnp.where(same_species, tall, 0.0).astype(BF16)
        all_species = groups * species
        wide = groups * width
        row_species = onehot(iota((wide, all_species), 0) // layers == iota((wide, all_species), 1))
        lane_species = onehot(iota((species, width), 0) == iota((species, width), 1) // layers)
        by_row = lax.dot_general(row_species, reaction_ref[...], NT, preferred_element_type=F32)
        spread_out = dot(by_row.astype(BF16), lane_species)
        same_layer = iota((wide, width), 0) % layers == iota((wide, width), 1) % layers
        mixer[...] = jnp.where(same_layer, spread_out, 0.0).astype(BF16)

    pl.semaphore_wait(barrier, len(partners))
    exchange(
        tile, spec, outer, send, stage, recv, [s.at[0] for s in sems], (under_first, under_second)
    )

    lane = iota((1, width), 1)
    left = lane < half
    rate = jnp.zeros((1, width), F32)
    for s in range(species):
        rate = rate + jnp.where(lane // layers == s, kappa_ref[0:1, s : s + 1], 0.0)
    thick_rows = jnp.dot(
        thickness_ref[...],
        jnp.where(iota((layers, width), 0) == iota((layers, width), 1) % layers, 1.0, 0.0),
        precision=HIGH,
        preferred_element_type=F32,
    )
    thick = jnp.zeros((1, width), F32)
    for s in range(species):
        thick = thick + jnp.where(lane // layers == s, thick_rows[s : s + 1, :], 0.0)

    digits = slots // RADIX
    digit = iota((digits, width), 0)

    def inject(o, injected):
        highs, wides = [], []
        for i in range(ROW):
            x = recv[o, i].astype(F32)
            highs.append(onehot(x[2:3, :].astype(jnp.int32) == digit))
            low_hit = x[3:4, :].astype(jnp.int32) == digit
            values = []
            for s in range(species):
                value = jnp.where(left if s % 2 == 0 else ~left, x[s // 2 : s // 2 + 1, :], 0.0)
                values.append(jnp.where(low_hit, value, 0.0).astype(BF16))
            wides.append(jnp.concatenate(values, axis=0))
        high_hot = jnp.concatenate(highs, axis=1)
        digit_hot[o] = high_hot
        return injected + lax.dot_general(
            jnp.concatenate(wides, axis=1),
            high_hot,
            NT,
            preferred_element_type=F32,
        )

    injected = lax.fori_loop(0, outer, inject, jnp.zeros((width, digits), F32)).T
    slot_digit = onehot(iota((slots, digits), 0) // RADIX == iota((slots, digits), 1))
    own_low = iota((slots, width), 0) % RADIX == iota((slots, width), 1) % RADIX
    block_ones = onehot(same_species)
    upper = injected.astype(BF16)
    lower = (injected - upper.astype(F32)).astype(BF16)
    added = jnp.zeros((slots, width), F32)
    for part in (upper, lower):
        chosen = jnp.where(own_low, dot(slot_digit, part), 0.0).astype(BF16)
        added = added + dot(chosen, block_ones)
    live = iota((slots, 1), 0) < count_ref[...]
    adjoint[...] = jnp.where(live, columns_ref[...].astype(F32) + thick * added, 0.0)

    keep = 1.0 - nbr_count * rate
    near = 2 * rim

    def launch(substep, outside):
        halo_out[substep] = outside.astype(BF16)
        copies = []
        for side, other in enumerate((previous, following)):
            copy = pltpu.make_async_remote_copy(
                src_ref=halo_out.at[substep, pl.ds(side * rim, rim)],
                dst_ref=halo_in.at[substep, pl.ds((1 - side) * rim, rim)],
                send_sem=halo_send.at[substep, side],
                recv_sem=halo_recv.at[substep, side],
                device_id=(other, spec),
                device_id_type=MESH,
            )
            copy.start()
            copies.append(copy)
        return copies

    spread = (rate * adjoint[...]).astype(BF16)
    copies = launch(0, dot(names[slots:, :], spread))
    adjoint[...] = keep * adjoint[...] + dot(names[0:slots, near:], spread[near:, :])
    spread_front = spread[0:near, :]
    for substep in range(SUB):
        bed = adjoint[near:, :] + dot(names[near:slots, 0:near], spread_front)
        rest = dot(bed.astype(BF16), operator[...])
        rims[...] = adjoint[0:near, :] + dot(names[0:near, 0:near], spread_front)
        if substep < SUB - 1:
            spread_rest = (rate * rest).astype(BF16)
            beyond[...] = dot(names[slots:, near:], spread_rest)
            adjoint[near:, :] = keep * rest + dot(names[near:slots, near:], spread_rest)
            adjoint[0:near, :] = dot(names[0:near, near:], spread_rest)
        else:
            gathered[spec, near:, :] = rest.astype(BF16)
        for copy in copies:
            copy.wait()
        front = rims[...] + halo_in[substep].astype(F32)
        front = dot(front.astype(BF16), operator[...])
        if substep < SUB - 1:
            spread_front = (rate * front).astype(BF16)
            copies = launch(substep + 1, beyond[...] + dot(names[slots:, 0:near], spread_front))
            adjoint[0:near, :] = adjoint[0:near, :] + keep * front
        else:
            gathered[spec, 0:near, :] = front.astype(BF16)

    own = gathered[spec]
    top_to_low = onehot(same_species & (iota((width, width), 0) % layers == 0))
    spread_top = jnp.where(own_low, dot(own, top_to_low), 0.0).astype(BF16)
    digit_slot = onehot(iota((digits, slots), 0) == iota((digits, slots), 1) // RADIX)
    tables[spec] = dot(digit_slot, spread_top).astype(BF16)

    def share(buffer, send_sem, recv_sem):
        copies = []
        for d, other in enumerate(peers):
            copy = pltpu.make_async_remote_copy(
                src_ref=buffer.at[spec],
                dst_ref=buffer.at[spec],
                send_sem=send_sem.at[d],
                recv_sem=recv_sem.at[d],
                device_id=(tile, other),
                device_id_type=MESH,
            )
            copy.start()
            copies.append(copy)
        return copies

    table_copies = share(tables, table_send, table_recv)

    right, left_peer = lax.rem(spec + 1, groups), lax.rem(spec + groups - 1, groups)
    middle = slots // 2

    def pass_on(origin, start, other, index):
        view = gathered.at[origin, pl.ds(start, middle)]
        copy = pltpu.make_async_remote_copy(
            src_ref=view,
            dst_ref=view,
            send_sem=gather_send.at[index],
            recv_sem=gather_recv.at[index],
            device_id=(tile, other),
            device_id_type=MESH,
        )
        copy.start()
        return copy

    to_right = pass_on(spec, 0, right, 0)
    to_left = pass_on(spec, middle, left_peer, 1)
    gather_copies = [pass_on(spec, middle, right, 2), pass_on(spec, 0, left_peer, 3)]

    def mixer_of(origin):
        return mixer[pl.ds(pl.multiple_of(origin * width, width), width), :]

    for copy in table_copies:
        copy.wait()
    table = jnp.zeros((digits, width), F32)
    for g in range(groups):
        table = table + dot(tables[g], mixer[g * width : (g + 1) * width, :])
    table = table.T.astype(BF16)

    def reply(o, carried):
        hits = []
        for i in range(ROW):
            x = recv[o, i].astype(F32)
            hits.append(x[3:4, :].astype(jnp.int32) == digit)
        found = dot(table, digit_hot[o])
        for i in range(ROW):
            lines = []
            for k in range(species // 2):
                even, odd = [
                    found[s * RADIX : (s + 1) * RADIX, i * width : (i + 1) * width]
                    for s in (2 * k, 2 * k + 1)
                ]
                picked = jnp.where(hits[i], jnp.where(left, even, odd), 0.0)
                lines.append(jnp.sum(picked, axis=0, keepdims=True))
            answer[o, i] = jnp.concatenate(lines, axis=0).astype(BF16)
        return carried

    lax.fori_loop(0, outer, reply, 0)

    def under_reply():
        to_right.wait()
        to_left.wait()
        gather_copies.append(pass_on(left_peer, 0, right, 4))
        gather_copies.append(pass_on(right, middle, left_peer, 5))

    def under_return():
        mixed = dot(own, mixer_of(spec))
        for copy in gather_copies:
            copy.wait()
        for d in range(1, groups):
            origin = lax.rem(spec + groups - d, groups)
            mixed = mixed + dot(gathered[origin], mixer_of(origin))
        state_ref[...] = mixed.astype(BF16)

    exchange(
        tile,
        spec,
        outer,
        answer,
        back,
        returned,
        [s.at[1] for s in sems],
        (under_reply, under_return),
    )
    for p in range(tiles):
        packed[2 * p : 2 * p + 2, :] = returned[p // ROW, p % ROW].astype(F32)
    by_place = jnp.concatenate(
        [packed[pl.ds(k, tiles, stride=2), :].T for k in range(species // 2)], axis=0
    ).astype(BF16)
    totals = [jnp.zeros((1, cells), F32) for _ in range(species)]
    for r in range(per_cell):
        owner = onehot(part_ref[r : r + 1, :] == iota((tiles, cells), 0))
        place = rank_ref[r : r + 1, :].astype(jnp.int32) == iota((half, cells), 0)
        found = dot(by_place, owner)
        for s in range(species):
            picked = jnp.where(place, found[s * half : (s + 1) * half, :], 0.0)
            picked = jnp.sum(picked, axis=0, keepdims=True)
            totals[s] = totals[s] + weight_ref[r : r + 1, :] * picked
    for s in range(species):
        bottom_ref[s : s + 1, :] = totals[s]


def whole():
    return pl.BlockSpec(memory_space=pltpu.VMEM)


def body(
    grad_columns,
    grad_flux,
    remap_part,
    remap_slot,
    remap_weight,
    col_count,
    neighbors,
    kappa,
    thickness,
    vertical,
    reaction,
):
    tiles, groups = lax.axis_size("tile"), lax.axis_size("spec")
    slots, width = grad_columns.shape
    species, layers = thickness.shape
    cells, per_cell = remap_part.shape
    rim = slots // 8
    outer = tiles // ROW
    digits = slots // RADIX
    nbr_count = neighbors.shape[1]
    dma = pltpu.SemaphoreType.DMA
    vmem = pltpu.VMEM
    grad_state, grad_bottom = pl.pallas_call(
        functools.partial(step_kernel, tiles, groups),
        out_shape=(
            jax.ShapeDtypeStruct((slots, width), BF16),
            jax.ShapeDtypeStruct((species, cells), F32),
        ),
        in_specs=[pl.BlockSpec(memory_space=pltpu.HBM)] * 11,
        out_specs=(whole(), whole()),
        scratch_shapes=[
            vmem((per_cell, cells), jnp.int32),
            vmem((per_cell, cells), jnp.int32),
            vmem((per_cell, cells), F32),
            vmem((species, cells), F32),
            vmem((slots, width), BF16),
            vmem((nbr_count, slots), jnp.int32),
            vmem((width, layers), BF16),
            vmem((species, layers), F32),
            vmem((1, 1), jnp.int32),
            vmem((1, species), F32),
            vmem((species, groups * species), BF16),
            vmem((per_cell, cells), F32),
            vmem((4 * tiles, width), F32),
            vmem((slots + 2 * rim, slots), BF16),
            vmem((slots, width), F32),
            vmem((width, width), BF16),
            vmem((groups * width, width), BF16),
            vmem((outer, ROW, 4, width), BF16),
            vmem((outer, ROW, 4, width), BF16),
            vmem((outer, ROW, 4, width), BF16),
            vmem((outer, ROW, 2, width), BF16),
            vmem((outer, ROW, 2, width), BF16),
            vmem((outer, ROW, 2, width), BF16),
            vmem((SUB, 2 * rim, width), BF16),
            vmem((SUB, 2 * rim, width), BF16),
            vmem((groups, slots, width), BF16),
            vmem((groups, digits, width), BF16),
            vmem((outer, digits, ROW * width), BF16),
            vmem((2 * rim, width), F32),
            vmem((2 * rim, width), F32),
            dma((11,)),
            dma((SUB, 2)),
            dma((SUB, 2)),
            dma((6,)),
            dma((6,)),
            dma((groups - 1,)),
            dma((groups - 1,)),
            dma((2, ROW - 1)),
            dma((2, ROW - 1)),
            dma((2, outer - 1)),
            dma((2, outer - 1)),
            dma((2, 2)),
        ],
        compiler_params=pltpu.CompilerParams(
            collective_id=0, has_side_effects=True, vmem_limit_bytes=60 * 2**20
        ),
        name="step",
    )(
        remap_part.T,
        remap_slot.T,
        remap_weight.T,
        grad_flux,
        grad_columns,
        neighbors.T,
        vertical.reshape(width, layers),
        thickness,
        col_count.reshape(1, 1),
        kappa.reshape(1, species),
        reaction.T,
    )
    return (grad_state, grad_bottom)


def solution(mesh):
    placed = (
        P("tile", "spec"),
        P("spec", "tile"),
        P("tile", None),
        P("tile", None),
        P("tile", None),
        P("tile"),
        P("tile", None),
        P("spec"),
        P("spec", None),
        P("spec", None, None),
        P(None, "spec"),
    )
    return jax.shard_map(
        body,
        mesh=mesh,
        in_specs=placed,
        out_specs=(P("tile", "spec"), P("spec", "tile")),
        check_vma=False,
    )
```

```python
import functools

import jax
import jax.numpy as jnp
from jax import lax
from jax.experimental import pallas as pl
from jax.experimental.pallas import tpu as pltpu
from jax.sharding import PartitionSpec as P

SUB = 4
F32 = jnp.float32
BF16 = jnp.bfloat16
MESH = pl.DeviceIdType.MESH
HIGH = lax.Precision.HIGHEST
NT = (((1,), (1,)), ((), ()))
RADIX = 32
ROW = 16


def dot(a, b):
    return jnp.dot(a, b, preferred_element_type=F32)


def iota(shape, dim):
    return lax.broadcasted_iota(jnp.int32, shape, dim)


def onehot(condition):
    return jnp.where(condition, 1.0, 0.0).astype(BF16)


def farthest_first(count):
    return sorted(range(1, count), key=lambda d: -min(d, count - d))


def swap_halves(x):
    half = x.shape[1] // 2
    return jnp.concatenate([x[:, half:], x[:, :half]], axis=1)


def exchange(tile, spec, outer, source, stage, target, sems, between):
    mine, row = lax.rem(tile, ROW), tile // ROW
    first_send, first_recv, second_send, second_recv, local = sems
    keep = pltpu.make_async_copy(source.at[:, mine], stage.at[:, mine], local.at[0])
    keep.start()
    copies = []
    for d in farthest_first(ROW):
        other = lax.rem(mine + d, ROW)
        copy = pltpu.make_async_remote_copy(
            src_ref=source.at[:, other],
            dst_ref=stage.at[:, mine],
            send_sem=first_send.at[d - 1],
            recv_sem=first_recv.at[d - 1],
            device_id=(row * ROW + other, spec),
            device_id_type=MESH,
        )
        copy.start()
        copies.append(copy)
    between[0]()
    keep.wait()
    for copy in copies:
        copy.wait()
    keep = pltpu.make_async_copy(stage.at[row], target.at[row], local.at[1])
    keep.start()
    copies = []
    for d in farthest_first(outer):
        other = lax.rem(row + d, outer)
        copy = pltpu.make_async_remote_copy(
            src_ref=stage.at[other],
            dst_ref=target.at[row],
            send_sem=second_send.at[d - 1],
            recv_sem=second_recv.at[d - 1],
            device_id=(other * ROW + mine, spec),
            device_id_type=MESH,
        )
        copy.start()
        copies.append(copy)
    between[1]()
    keep.wait()
    for copy in copies:
        copy.wait()


def step_kernel(
    tiles,
    groups,
    part_hbm,
    slot_hbm,
    weight_hbm,
    flux_hbm,
    columns_hbm,
    neighbors_hbm,
    vertical_hbm,
    thickness_hbm,
    count_hbm,
    kappa_hbm,
    reaction_hbm,
    state_ref,
    bottom_ref,
    part_ref,
    slot_ref,
    weight_ref,
    flux_ref,
    columns_ref,
    neighbors_ref,
    vertical_ref,
    thickness_ref,
    count_ref,
    kappa_ref,
    reaction_ref,
    rank_ref,
    packed,
    names,
    adjoint,
    operator,
    mixer,
    send,
    stage,
    recv,
    answer,
    back,
    returned,
    halo_out,
    halo_in,
    gathered,
    tables,
    digit_hot,
    rims,
    beyond,
    load_sem,
    halo_send,
    halo_recv,
    gather_send,
    gather_recv,
    table_send,
    table_recv,
    *sems,
):
    slots, width = columns_ref.shape
    species, layers = thickness_ref.shape
    per_cell, cells = part_ref.shape
    outer = tiles // ROW
    half = width // 2
    rim = slots // 8
    nbr_count = neighbors_ref.shape[0]
    tile, spec = lax.axis_index("tile"), lax.axis_index("spec")
    mine, row = lax.rem(tile, ROW), tile // ROW
    following = lax.rem(tile + 1, tiles)
    previous = lax.rem(tile + tiles - 1, tiles)
    peers = [lax.rem(spec + d, groups) for d in range(1, groups)]

    loads = []
    for k, (src, dst) in enumerate(
        (
            (part_hbm, part_ref),
            (slot_hbm, slot_ref),
            (weight_hbm, weight_ref),
            (flux_hbm, flux_ref),
            (neighbors_hbm, neighbors_ref),
            (columns_hbm, columns_ref),
            (vertical_hbm, vertical_ref),
            (thickness_hbm, thickness_ref),
            (count_hbm, count_ref),
            (kappa_hbm, kappa_ref),
            (reaction_hbm, reaction_ref),
        )
    ):
        load = pltpu.make_async_copy(src, dst, load_sem.at[k])
        load.start()
        loads.append(load)

    barrier = pltpu.get_barrier_semaphore()
    partners = [(other, spec) for other in (previous, following)]
    partners += [(tile, other) for other in peers]
    partners += [(row * ROW + lax.rem(mine + d, ROW), spec) for d in range(1, ROW)]
    partners += [(lax.rem(row + d, outer) * ROW + mine, spec) for d in range(1, outer)]
    for partner in partners:
        pl.semaphore_signal(barrier, inc=1, device_id=partner, device_id_type=MESH)

    for load in loads[:4]:
        load.wait()
    chunk = 256
    before = onehot(iota((chunk, chunk), 0) < iota((chunk, chunk), 1))
    carry = jnp.zeros((tiles, 1), F32)
    total = jnp.zeros((tiles, 4 * width), F32)
    for r in range(per_cell):
        hit = part_ref[r : r + 1, :] == iota((tiles, cells), 0)
        owner = jnp.where(hit, 1.0, 0.0)
        owner_b = owner.astype(BF16)
        for k in range(0, cells, chunk):
            piece = owner[:, k : k + chunk]
            earlier = dot(owner_b[:, k : k + chunk], before) + carry
            rank_ref[r : r + 1, k : k + chunk] = jnp.sum(piece * earlier, axis=0, keepdims=True)
            carry = carry + jnp.sum(piece, axis=1, keepdims=True)
        place = rank_ref[r : r + 1, :].astype(jnp.int32) == iota((half, cells), 0)
        slot = slot_ref[r : r + 1, :]
        weight = weight_ref[r : r + 1, :]
        rows = [weight * flux_ref[s : s + 1, :] for s in range(species)]
        rows.append((slot // RADIX).astype(F32))
        rows.append((slot % RADIX).astype(F32))
        pieces = [jnp.where(place, value, 0.0).astype(BF16) for value in rows]
        pieces = pieces[:5] + pieces[4:] + pieces[5:]
        wide = jnp.concatenate(pieces, axis=0)
        total = total + lax.dot_general(owner_b, wide, NT, preferred_element_type=F32)
    for k in range(4):
        packed[pl.ds(k, tiles, stride=4), :] = total[:, k * width : (k + 1) * width]
    for d in range(tiles):
        send[d // ROW, d % ROW] = packed[4 * d : 4 * d + 4, :].astype(BF16)

    step = 256

    def name(m):
        code = iota((step, slots), 0) + m
        count = jnp.zeros((step, slots), F32)
        for n in range(nbr_count):
            count = count + jnp.where(neighbors_ref[n : n + 1, :] == code, 1.0, 0.0)
        names[m : m + step, :] = count.astype(BF16)

    def under_first():
        loads[4].wait()
        for m in range(0, 3 * step, step):
            name(m)

    same_species = iota((width, width), 0) // layers == iota((width, width), 1) // layers

    def under_second():
        for m in range(3 * step, slots + 2 * rim, step):
            name(m)
        layer_to_lane = onehot(iota((layers, width), 0) == iota((layers, width), 1) % layers)
        for load in loads[5:]:
            load.wait()
        tall = dot(vertical_ref[...], layer_to_lane)
        operator[...] = jnp.where(same_species, tall, 0.0).astype(BF16)
        all_species = groups * species
        wide = groups * width
        row_species = onehot(iota((wide, all_species), 0) // layers == iota((wide, all_species), 1))
        lane_species = onehot(iota((species, width), 0) == iota((species, width), 1) // layers)
        by_row = lax.dot_general(row_species, reaction_ref[...], NT, preferred_element_type=F32)
        spread_out = dot(by_row.astype(BF16), lane_species)
        same_layer = iota((wide, width), 0) % layers == iota((wide, width), 1) % layers
        mixer[...] = jnp.where(same_layer, spread_out, 0.0).astype(BF16)

    pl.semaphore_wait(barrier, len(partners))
    exchange(
        tile, spec, outer, send, stage, recv, [s.at[0] for s in sems], (under_first, under_second)
    )

    lane = iota((1, width), 1)
    left = lane < half
    rate = jnp.zeros((1, width), F32)
    for s in range(species):
        rate = rate + jnp.where(lane // layers == s, kappa_ref[0:1, s : s + 1], 0.0)
    thick_rows = jnp.dot(
        thickness_ref[...],
        jnp.where(iota((layers, width), 0) == iota((layers, width), 1) % layers, 1.0, 0.0),
        precision=HIGH,
        preferred_element_type=F32,
    )
    thick = jnp.zeros((1, width), F32)
    for s in range(species):
        thick = thick + jnp.where(lane // layers == s, thick_rows[s : s + 1, :], 0.0)

    digits = slots // RADIX
    digit = iota((digits, width), 0)

    def inject(o, injected):
        highs, wides = [], []
        for i in range(0, ROW, 2):
            one, two = recv[o, i].astype(F32), recv[o, i + 1].astype(F32)
            slots_of = jnp.where(left, one, two)
            evens = jnp.where(left, one, swap_halves(two))
            odds = jnp.where(left, swap_halves(one), two)
            highs.append(onehot(slots_of[2:3, :].astype(jnp.int32) == digit))
            low_hit = slots_of[3:4, :].astype(jnp.int32) == digit
            values = []
            for s in range(species):
                value = (evens if s % 2 == 0 else odds)[s // 2 : s // 2 + 1, :]
                values.append(jnp.where(low_hit, value, 0.0).astype(BF16))
            wides.append(jnp.concatenate(values, axis=0))
        high_hot = jnp.concatenate(highs, axis=1)
        digit_hot[o] = high_hot
        return injected + lax.dot_general(
            jnp.concatenate(wides, axis=1),
            high_hot,
            NT,
            preferred_element_type=F32,
        )

    injected = lax.fori_loop(0, outer, inject, jnp.zeros((width, digits), F32)).T
    slot_digit = onehot(iota((slots, digits), 0) // RADIX == iota((slots, digits), 1))
    own_low = iota((slots, width), 0) % RADIX == iota((slots, width), 1) % RADIX
    block_ones = onehot(same_species)
    upper = injected.astype(BF16)
    lower = (injected - upper.astype(F32)).astype(BF16)
    added = jnp.zeros((slots, width), F32)
    for part in (upper, lower):
        chosen = jnp.where(own_low, dot(slot_digit, part), 0.0).astype(BF16)
        added = added + dot(chosen, block_ones)
    live = iota((slots, 1), 0) < count_ref[...]
    adjoint[...] = jnp.where(live, columns_ref[...].astype(F32) + thick * added, 0.0)

    keep = 1.0 - nbr_count * rate
    near = 2 * rim

    def launch(substep, outside):
        halo_out[substep] = outside.astype(BF16)
        copies = []
        for side, other in enumerate((previous, following)):
            copy = pltpu.make_async_remote_copy(
                src_ref=halo_out.at[substep, pl.ds(side * rim, rim)],
                dst_ref=halo_in.at[substep, pl.ds((1 - side) * rim, rim)],
                send_sem=halo_send.at[substep, side],
                recv_sem=halo_recv.at[substep, side],
                device_id=(other, spec),
                device_id_type=MESH,
            )
            copy.start()
            copies.append(copy)
        return copies

    spread = (rate * adjoint[...]).astype(BF16)
    copies = launch(0, dot(names[slots:, :], spread))
    adjoint[...] = keep * adjoint[...] + dot(names[0:slots, near:], spread[near:, :])
    spread_front = spread[0:near, :]
    for substep in range(SUB):
        bed = adjoint[near:, :] + dot(names[near:slots, 0:near], spread_front)
        rest = dot(bed.astype(BF16), operator[...])
        rims[...] = adjoint[0:near, :] + dot(names[0:near, 0:near], spread_front)
        if substep < SUB - 1:
            spread_rest = (rate * rest).astype(BF16)
            beyond[...] = dot(names[slots:, near:], spread_rest)
            adjoint[near:, :] = keep * rest + dot(names[near:slots, near:], spread_rest)
            adjoint[0:near, :] = dot(names[0:near, near:], spread_rest)
        else:
            gathered[spec, near:, :] = rest.astype(BF16)
        for copy in copies:
            copy.wait()
        front = rims[...] + halo_in[substep].astype(F32)
        front = dot(front.astype(BF16), operator[...])
        if substep < SUB - 1:
            spread_front = (rate * front).astype(BF16)
            copies = launch(substep + 1, beyond[...] + dot(names[slots:, 0:near], spread_front))
            adjoint[0:near, :] = adjoint[0:near, :] + keep * front
        else:
            gathered[spec, 0:near, :] = front.astype(BF16)

    own = gathered[spec]
    top_to_low = onehot(same_species & (iota((width, width), 0) % layers == 0))
    spread_top = jnp.where(own_low, dot(own, top_to_low), 0.0).astype(BF16)
    digit_slot = onehot(iota((digits, slots), 0) == iota((digits, slots), 1) // RADIX)
    tables[spec] = dot(digit_slot, spread_top).astype(BF16)

    def share(buffer, send_sem, recv_sem):
        copies = []
        for d, other in enumerate(peers):
            copy = pltpu.make_async_remote_copy(
                src_ref=buffer.at[spec],
                dst_ref=buffer.at[spec],
                send_sem=send_sem.at[d],
                recv_sem=recv_sem.at[d],
                device_id=(tile, other),
                device_id_type=MESH,
            )
            copy.start()
            copies.append(copy)
        return copies

    table_copies = share(tables, table_send, table_recv)

    right, left_peer = lax.rem(spec + 1, groups), lax.rem(spec + groups - 1, groups)
    middle = slots // 2

    def pass_on(origin, start, other, index):
        view = gathered.at[origin, pl.ds(start, middle)]
        copy = pltpu.make_async_remote_copy(
            src_ref=view,
            dst_ref=view,
            send_sem=gather_send.at[index],
            recv_sem=gather_recv.at[index],
            device_id=(tile, other),
            device_id_type=MESH,
        )
        copy.start()
        return copy

    to_right = pass_on(spec, 0, right, 0)
    to_left = pass_on(spec, middle, left_peer, 1)
    gather_copies = [pass_on(spec, middle, right, 2), pass_on(spec, 0, left_peer, 3)]

    def mixer_of(origin):
        return mixer[pl.ds(pl.multiple_of(origin * width, width), width), :]

    for copy in table_copies:
        copy.wait()
    table = jnp.zeros((digits, width), F32)
    for g in range(groups):
        table = table + dot(tables[g], mixer[g * width : (g + 1) * width, :])
    table = table.T.astype(BF16)

    def reply(o, carried):
        found = dot(table, digit_hot[o])
        for i in range(0, ROW, 2):
            one, two = recv[o, i].astype(F32), recv[o, i + 1].astype(F32)
            low_hit = jnp.where(left, one, two)[3:4, :].astype(jnp.int32) == digit
            lines = []
            for s in range(species):
                block = found[s * RADIX : (s + 1) * RADIX, i // 2 * width : (i // 2 + 1) * width]
                lines.append(jnp.sum(jnp.where(low_hit, block, 0.0), axis=0, keepdims=True))
            evens = jnp.concatenate(lines[0::2], axis=0)
            odds = jnp.concatenate(lines[1::2], axis=0)
            answer[o, i] = jnp.where(left, evens, swap_halves(odds)).astype(BF16)
            answer[o, i + 1] = jnp.where(left, swap_halves(evens), odds).astype(BF16)
        return carried

    lax.fori_loop(0, outer, reply, 0)

    def under_reply():
        to_right.wait()
        to_left.wait()
        gather_copies.append(pass_on(left_peer, 0, right, 4))
        gather_copies.append(pass_on(right, middle, left_peer, 5))

    def under_return():
        mixed = dot(own, mixer_of(spec))
        for copy in gather_copies:
            copy.wait()
        for d in range(1, groups):
            origin = lax.rem(spec + groups - d, groups)
            mixed = mixed + dot(gathered[origin], mixer_of(origin))
        state_ref[...] = mixed.astype(BF16)

    exchange(
        tile,
        spec,
        outer,
        answer,
        back,
        returned,
        [s.at[1] for s in sems],
        (under_reply, under_return),
    )
    for p in range(tiles):
        packed[2 * p : 2 * p + 2, :] = returned[p // ROW, p % ROW].astype(F32)
    by_place = jnp.concatenate(
        [packed[pl.ds(k, tiles, stride=2), :].T for k in range(species // 2)], axis=0
    ).astype(BF16)
    totals = [jnp.zeros((1, cells), F32) for _ in range(species)]
    for r in range(per_cell):
        owner = onehot(part_ref[r : r + 1, :] == iota((tiles, cells), 0))
        place = rank_ref[r : r + 1, :].astype(jnp.int32) == iota((half, cells), 0)
        found = dot(by_place, owner)
        for s in range(species):
            picked = jnp.where(place, found[s * half : (s + 1) * half, :], 0.0)
            picked = jnp.sum(picked, axis=0, keepdims=True)
            totals[s] = totals[s] + weight_ref[r : r + 1, :] * picked
    for s in range(species):
        bottom_ref[s : s + 1, :] = totals[s]


def whole():
    return pl.BlockSpec(memory_space=pltpu.VMEM)


def body(
    grad_columns,
    grad_flux,
    remap_part,
    remap_slot,
    remap_weight,
    col_count,
    neighbors,
    kappa,
    thickness,
    vertical,
    reaction,
):
    tiles, groups = lax.axis_size("tile"), lax.axis_size("spec")
    slots, width = grad_columns.shape
    species, layers = thickness.shape
    cells, per_cell = remap_part.shape
    rim = slots // 8
    outer = tiles // ROW
    digits = slots // RADIX
    nbr_count = neighbors.shape[1]
    dma = pltpu.SemaphoreType.DMA
    vmem = pltpu.VMEM
    grad_state, grad_bottom = pl.pallas_call(
        functools.partial(step_kernel, tiles, groups),
        out_shape=(
            jax.ShapeDtypeStruct((slots, width), BF16),
            jax.ShapeDtypeStruct((species, cells), F32),
        ),
        in_specs=[pl.BlockSpec(memory_space=pltpu.HBM)] * 11,
        out_specs=(whole(), whole()),
        scratch_shapes=[
            vmem((per_cell, cells), jnp.int32),
            vmem((per_cell, cells), jnp.int32),
            vmem((per_cell, cells), F32),
            vmem((species, cells), F32),
            vmem((slots, width), BF16),
            vmem((nbr_count, slots), jnp.int32),
            vmem((width, layers), BF16),
            vmem((species, layers), F32),
            vmem((1, 1), jnp.int32),
            vmem((1, species), F32),
            vmem((species, groups * species), BF16),
            vmem((per_cell, cells), F32),
            vmem((4 * tiles, width), F32),
            vmem((slots + 2 * rim, slots), BF16),
            vmem((slots, width), F32),
            vmem((width, width), BF16),
            vmem((groups * width, width), BF16),
            vmem((outer, ROW, 4, width), BF16),
            vmem((outer, ROW, 4, width), BF16),
            vmem((outer, ROW, 4, width), BF16),
            vmem((outer, ROW, 2, width), BF16),
            vmem((outer, ROW, 2, width), BF16),
            vmem((outer, ROW, 2, width), BF16),
            vmem((SUB, 2 * rim, width), BF16),
            vmem((SUB, 2 * rim, width), BF16),
            vmem((groups, slots, width), BF16),
            vmem((groups, digits, width), BF16),
            vmem((outer, digits, ROW // 2 * width), BF16),
            vmem((2 * rim, width), F32),
            vmem((2 * rim, width), F32),
            dma((11,)),
            dma((SUB, 2)),
            dma((SUB, 2)),
            dma((6,)),
            dma((6,)),
            dma((groups - 1,)),
            dma((groups - 1,)),
            dma((2, ROW - 1)),
            dma((2, ROW - 1)),
            dma((2, outer - 1)),
            dma((2, outer - 1)),
            dma((2, 2)),
        ],
        compiler_params=pltpu.CompilerParams(
            collective_id=0, has_side_effects=True, vmem_limit_bytes=60 * 2**20
        ),
        name="step",
    )(
        remap_part.T,
        remap_slot.T,
        remap_weight.T,
        grad_flux,
        grad_columns,
        neighbors.T,
        vertical.reshape(width, layers),
        thickness,
        col_count.reshape(1, 1),
        kappa.reshape(1, species),
        reaction.T,
    )
    return (grad_state, grad_bottom)


def solution(mesh):
    placed = (
        P("tile", "spec"),
        P("spec", "tile"),
        P("tile", None),
        P("tile", None),
        P("tile", None),
        P("tile"),
        P("tile", None),
        P("spec"),
        P("spec", None),
        P("spec", None, None),
        P(None, "spec"),
    )
    return jax.shard_map(
        body,
        mesh=mesh,
        in_specs=placed,
        out_specs=(P("tile", "spec"), P("spec", "tile")),
        check_vma=False,
    )
```

```python
import functools

import jax
import jax.numpy as jnp
from jax import lax
from jax.experimental import pallas as pl
from jax.experimental.pallas import tpu as pltpu
from jax.sharding import PartitionSpec as P

SUB = 4
F32 = jnp.float32
BF16 = jnp.bfloat16
MESH = pl.DeviceIdType.MESH
HIGH = lax.Precision.HIGHEST
NT = (((1,), (1,)), ((), ()))
RADIX = 32
ROW = 16


def dot(a, b):
    return jnp.dot(a, b, preferred_element_type=F32)


def iota(shape, dim):
    return lax.broadcasted_iota(jnp.int32, shape, dim)


def onehot(condition):
    return jnp.where(condition, 1.0, 0.0).astype(BF16)


def farthest_first(count):
    return sorted(range(1, count), key=lambda d: -min(d, count - d))


def swap_halves(x):
    half = x.shape[1] // 2
    return jnp.concatenate([x[:, half:], x[:, :half]], axis=1)


def exchange(tile, spec, outer, source, stage, target, sems, between):
    mine, row = lax.rem(tile, ROW), tile // ROW
    first_send, first_recv, second_send, second_recv, local = sems
    keep = pltpu.make_async_copy(source.at[:, mine], stage.at[:, mine], local.at[0])
    keep.start()
    copies = []
    for d in farthest_first(ROW):
        other = lax.rem(mine + d, ROW)
        copy = pltpu.make_async_remote_copy(
            src_ref=source.at[:, other],
            dst_ref=stage.at[:, mine],
            send_sem=first_send.at[d - 1],
            recv_sem=first_recv.at[d - 1],
            device_id=(row * ROW + other, spec),
            device_id_type=MESH,
        )
        copy.start()
        copies.append(copy)
    between[0]()
    keep.wait()
    for copy in copies:
        copy.wait()
    keep = pltpu.make_async_copy(stage.at[row], target.at[row], local.at[1])
    keep.start()
    copies = []
    for d in farthest_first(outer):
        other = lax.rem(row + d, outer)
        copy = pltpu.make_async_remote_copy(
            src_ref=stage.at[other],
            dst_ref=target.at[row],
            send_sem=second_send.at[d - 1],
            recv_sem=second_recv.at[d - 1],
            device_id=(other * ROW + mine, spec),
            device_id_type=MESH,
        )
        copy.start()
        copies.append(copy)
    between[1]()
    keep.wait()
    for copy in copies:
        copy.wait()


def step_kernel(
    tiles,
    groups,
    part_hbm,
    slot_hbm,
    weight_hbm,
    flux_hbm,
    columns_hbm,
    neighbors_hbm,
    vertical_hbm,
    thickness_hbm,
    count_hbm,
    kappa_hbm,
    reaction_hbm,
    state_ref,
    bottom_ref,
    part_ref,
    slot_ref,
    weight_ref,
    flux_ref,
    columns_ref,
    neighbors_ref,
    vertical_ref,
    thickness_ref,
    count_ref,
    kappa_ref,
    reaction_ref,
    rank_ref,
    packed,
    names,
    adjoint,
    operator,
    mixer,
    send,
    stage,
    recv,
    answer,
    back,
    returned,
    halo_out,
    halo_in,
    gathered,
    tables,
    digit_hot,
    rims,
    beyond,
    load_sem,
    halo_send,
    halo_recv,
    gather_send,
    gather_recv,
    table_send,
    table_recv,
    *sems,
):
    slots, width = columns_ref.shape
    species, layers = thickness_ref.shape
    per_cell, cells = part_ref.shape
    outer = tiles // ROW
    half = width // 2
    rim = slots // 8
    nbr_count = neighbors_ref.shape[0]
    tile, spec = lax.axis_index("tile"), lax.axis_index("spec")
    mine, row = lax.rem(tile, ROW), tile // ROW
    following = lax.rem(tile + 1, tiles)
    previous = lax.rem(tile + tiles - 1, tiles)
    peers = [lax.rem(spec + d, groups) for d in range(1, groups)]

    loads = []
    for k, (src, dst) in enumerate(
        (
            (part_hbm, part_ref),
            (slot_hbm, slot_ref),
            (weight_hbm, weight_ref),
            (flux_hbm, flux_ref),
            (neighbors_hbm, neighbors_ref),
            (columns_hbm, columns_ref),
            (vertical_hbm, vertical_ref),
            (thickness_hbm, thickness_ref),
            (count_hbm, count_ref),
            (kappa_hbm, kappa_ref),
            (reaction_hbm, reaction_ref),
        )
    ):
        load = pltpu.make_async_copy(src, dst, load_sem.at[k])
        load.start()
        loads.append(load)

    barrier = pltpu.get_barrier_semaphore()
    partners = [(other, spec) for other in (previous, following)]
    partners += [(tile, other) for other in peers]
    partners += [(row * ROW + lax.rem(mine + d, ROW), spec) for d in range(1, ROW)]
    partners += [(lax.rem(row + d, outer) * ROW + mine, spec) for d in range(1, outer)]
    for partner in partners:
        pl.semaphore_signal(barrier, inc=1, device_id=partner, device_id_type=MESH)

    for load in loads[:4]:
        load.wait()
    chunk = 256
    before = onehot(iota((chunk, chunk), 0) < iota((chunk, chunk), 1))
    carry = jnp.zeros((tiles, 1), F32)
    total = jnp.zeros((tiles, 4 * width), F32)
    for r in range(per_cell):
        hit = part_ref[r : r + 1, :] == iota((tiles, cells), 0)
        owner = jnp.where(hit, 1.0, 0.0)
        owner_b = owner.astype(BF16)
        for k in range(0, cells, chunk):
            piece = owner[:, k : k + chunk]
            earlier = dot(owner_b[:, k : k + chunk], before) + carry
            rank_ref[r : r + 1, k : k + chunk] = jnp.sum(piece * earlier, axis=0, keepdims=True)
            carry = carry + jnp.sum(piece, axis=1, keepdims=True)
        place = rank_ref[r : r + 1, :].astype(jnp.int32) == iota((half, cells), 0)
        slot = slot_ref[r : r + 1, :]
        weight = weight_ref[r : r + 1, :]
        rows = [weight * flux_ref[s : s + 1, :] for s in range(species)]
        rows.append((slot // RADIX).astype(F32))
        rows.append((slot % RADIX).astype(F32))
        pieces = [jnp.where(place, value, 0.0).astype(BF16) for value in rows]
        pieces = pieces[:5] + pieces[4:] + pieces[5:]
        wide = jnp.concatenate(pieces, axis=0)
        total = total + lax.dot_general(owner_b, wide, NT, preferred_element_type=F32)
    for k in range(4):
        packed[pl.ds(k, tiles, stride=4), :] = total[:, k * width : (k + 1) * width]
    for d in range(tiles):
        send[d // ROW, d % ROW] = packed[4 * d : 4 * d + 4, :].astype(BF16)

    step = 256

    def name(m):
        code = iota((step, slots), 0) + m
        count = jnp.zeros((step, slots), F32)
        for n in range(nbr_count):
            count = count + jnp.where(neighbors_ref[n : n + 1, :] == code, 1.0, 0.0)
        names[m : m + step, :] = count.astype(BF16)

    def under_first():
        loads[4].wait()
        for m in range(0, 3 * step, step):
            name(m)

    same_species = iota((width, width), 0) // layers == iota((width, width), 1) // layers

    def under_second():
        for m in range(3 * step, slots + 2 * rim, step):
            name(m)
        layer_to_lane = onehot(iota((layers, width), 0) == iota((layers, width), 1) % layers)
        for load in loads[5:]:
            load.wait()
        tall = dot(vertical_ref[...], layer_to_lane)
        operator[...] = jnp.where(same_species, tall, 0.0).astype(BF16)
        all_species = groups * species
        wide = groups * width
        row_species = onehot(iota((wide, all_species), 0) // layers == iota((wide, all_species), 1))
        lane_species = onehot(iota((species, width), 0) == iota((species, width), 1) // layers)
        by_row = lax.dot_general(row_species, reaction_ref[...], NT, preferred_element_type=F32)
        spread_out = dot(by_row.astype(BF16), lane_species)
        same_layer = iota((wide, width), 0) % layers == iota((wide, width), 1) % layers
        mixer[...] = jnp.where(same_layer, spread_out, 0.0).astype(BF16)

    pl.semaphore_wait(barrier, len(partners))
    exchange(
        tile, spec, outer, send, stage, recv, [s.at[0] for s in sems], (under_first, under_second)
    )

    lane = iota((1, width), 1)
    left = lane < half
    rate = jnp.zeros((1, width), F32)
    for s in range(species):
        rate = rate + jnp.where(lane // layers == s, kappa_ref[0:1, s : s + 1], 0.0)
    thick_rows = jnp.dot(
        thickness_ref[...],
        jnp.where(iota((layers, width), 0) == iota((layers, width), 1) % layers, 1.0, 0.0),
        precision=HIGH,
        preferred_element_type=F32,
    )
    thick = jnp.zeros((1, width), F32)
    for s in range(species):
        thick = thick + jnp.where(lane // layers == s, thick_rows[s : s + 1, :], 0.0)

    digits = slots // RADIX
    digit = iota((digits, width), 0)

    def inject(o, injected):
        highs, wides = [], []
        for i in range(0, ROW, 2):
            one, two = recv[o, i].astype(F32), recv[o, i + 1].astype(F32)
            slots_of = jnp.where(left, one, two)
            evens = jnp.where(left, one, swap_halves(two))
            odds = jnp.where(left, swap_halves(one), two)
            highs.append(onehot(slots_of[2:3, :].astype(jnp.int32) == digit))
            low_hit = slots_of[3:4, :].astype(jnp.int32) == digit
            values = []
            for s in range(species):
                value = (evens if s % 2 == 0 else odds)[s // 2 : s // 2 + 1, :]
                values.append(jnp.where(low_hit, value, 0.0).astype(BF16))
            wides.append(jnp.concatenate(values, axis=0))
        high_hot = jnp.concatenate(highs, axis=1)
        digit_hot[o] = high_hot
        return injected + lax.dot_general(
            jnp.concatenate(wides, axis=1),
            high_hot,
            NT,
            preferred_element_type=F32,
        )

    injected = lax.fori_loop(0, outer, inject, jnp.zeros((width, digits), F32)).T
    slot_digit = onehot(iota((slots, digits), 0) // RADIX == iota((slots, digits), 1))
    own_low = iota((slots, width), 0) % RADIX == iota((slots, width), 1) % RADIX
    block_ones = onehot(same_species)
    upper = injected.astype(BF16)
    lower = (injected - upper.astype(F32)).astype(BF16)
    added = jnp.zeros((slots, width), F32)
    for part in (upper, lower):
        chosen = jnp.where(own_low, dot(slot_digit, part), 0.0).astype(BF16)
        added = added + dot(chosen, block_ones)
    live = iota((slots, 1), 0) < count_ref[...]
    adjoint[...] = jnp.where(live, columns_ref[...].astype(F32) + thick * added, 0.0)

    keep = 1.0 - nbr_count * rate
    near = 2 * rim

    def launch(substep, outside):
        halo_out[substep] = outside.astype(BF16)
        copies = []
        for side, other in enumerate((previous, following)):
            copy = pltpu.make_async_remote_copy(
                src_ref=halo_out.at[substep, pl.ds(side * rim, rim)],
                dst_ref=halo_in.at[substep, pl.ds((1 - side) * rim, rim)],
                send_sem=halo_send.at[substep, side],
                recv_sem=halo_recv.at[substep, side],
                device_id=(other, spec),
                device_id_type=MESH,
            )
            copy.start()
            copies.append(copy)
        return copies

    spread = (rate * adjoint[...]).astype(BF16)
    copies = launch(0, dot(names[slots:, :], spread))
    adjoint[...] = keep * adjoint[...] + dot(names[0:slots, near:], spread[near:, :])
    spread_front = spread[0:near, :]
    for substep in range(SUB):
        bed = adjoint[near:, :] + dot(names[near:slots, 0:near], spread_front)
        rest = dot(bed.astype(BF16), operator[...])
        rims[...] = adjoint[0:near, :] + dot(names[0:near, 0:near], spread_front)
        if substep < SUB - 1:
            spread_rest = (rate * rest).astype(BF16)
            beyond[...] = dot(names[slots:, near:], spread_rest)
            adjoint[near:, :] = keep * rest + dot(names[near:slots, near:], spread_rest)
            adjoint[0:near, :] = dot(names[0:near, near:], spread_rest)
        else:
            gathered[spec, near:, :] = rest.astype(BF16)
        for copy in copies:
            copy.wait()
        front = rims[...] + halo_in[substep].astype(F32)
        front = dot(front.astype(BF16), operator[...])
        if substep < SUB - 1:
            spread_front = (rate * front).astype(BF16)
            copies = launch(substep + 1, beyond[...] + dot(names[slots:, 0:near], spread_front))
            adjoint[0:near, :] = adjoint[0:near, :] + keep * front
        else:
            gathered[spec, 0:near, :] = front.astype(BF16)

    own = gathered[spec]
    top_to_low = onehot(same_species & (iota((width, width), 0) % layers == 0))
    spread_top = jnp.where(own_low, dot(own, top_to_low), 0.0).astype(BF16)
    digit_slot = onehot(iota((digits, slots), 0) == iota((digits, slots), 1) // RADIX)
    tables[spec] = dot(digit_slot, spread_top).astype(BF16)

    def share(buffer, send_sem, recv_sem):
        copies = []
        for d, other in enumerate(peers):
            copy = pltpu.make_async_remote_copy(
                src_ref=buffer.at[spec],
                dst_ref=buffer.at[spec],
                send_sem=send_sem.at[d],
                recv_sem=recv_sem.at[d],
                device_id=(tile, other),
                device_id_type=MESH,
            )
            copy.start()
            copies.append(copy)
        return copies

    table_copies = share(tables, table_send, table_recv)

    right, left_peer = lax.rem(spec + 1, groups), lax.rem(spec + groups - 1, groups)
    middle = slots // 2

    def pass_on(origin, start, other, index):
        view = gathered.at[origin, pl.ds(start, middle)]
        copy = pltpu.make_async_remote_copy(
            src_ref=view,
            dst_ref=view,
            send_sem=gather_send.at[index],
            recv_sem=gather_recv.at[index],
            device_id=(tile, other),
            device_id_type=MESH,
        )
        copy.start()
        return copy

    to_right = pass_on(spec, 0, right, 0)
    to_left = pass_on(spec, middle, left_peer, 1)
    gather_copies = [pass_on(spec, middle, right, 2), pass_on(spec, 0, left_peer, 3)]

    def mixer_of(origin):
        return mixer[pl.ds(pl.multiple_of(origin * width, width), width), :]

    for copy in table_copies:
        copy.wait()
    table = jnp.zeros((digits, width), F32)
    for g in range(groups):
        table = table + dot(tables[g], mixer[g * width : (g + 1) * width, :])
    table = table.T.astype(BF16)

    def reply(o, carried):
        found = dot(table, digit_hot[o])
        for i in range(0, ROW, 2):
            one, two = recv[o, i].astype(F32), recv[o, i + 1].astype(F32)
            low_hit = jnp.where(left, one, two)[3:4, :].astype(jnp.int32) == digit
            lines = []
            for s in range(species):
                block = found[s * RADIX : (s + 1) * RADIX, i // 2 * width : (i // 2 + 1) * width]
                lines.append(jnp.sum(jnp.where(low_hit, block, 0.0), axis=0, keepdims=True))
            evens = jnp.concatenate(lines[0::2], axis=0)
            odds = jnp.concatenate(lines[1::2], axis=0)
            answer[o, i] = jnp.where(left, evens, swap_halves(odds)).astype(BF16)
            answer[o, i + 1] = jnp.where(left, swap_halves(evens), odds).astype(BF16)
        return carried

    lax.fori_loop(0, outer, reply, 0)

    def under_reply():
        to_right.wait()
        to_left.wait()
        gather_copies.append(pass_on(left_peer, 0, right, 4))
        gather_copies.append(pass_on(right, middle, left_peer, 5))

    def under_return():
        mixed = dot(own, mixer_of(spec))
        for copy in gather_copies:
            copy.wait()
        for d in range(1, groups):
            origin = lax.rem(spec + groups - d, groups)
            mixed = mixed + dot(gathered[origin], mixer_of(origin))
        state_ref[...] = mixed.astype(BF16)

    exchange(
        tile,
        spec,
        outer,
        answer,
        back,
        returned,
        [s.at[1] for s in sems],
        (under_reply, under_return),
    )
    for p in range(tiles):
        packed[2 * p : 2 * p + 2, :] = returned[p // ROW, p % ROW].astype(F32)
    by_place = jnp.concatenate(
        [packed[pl.ds(k, tiles, stride=2), :].T for k in range(species // 2)], axis=0
    ).astype(BF16)
    totals = [jnp.zeros((1, cells), F32) for _ in range(species)]
    for r in range(per_cell):
        owner = onehot(part_ref[r : r + 1, :] == iota((tiles, cells), 0))
        place = rank_ref[r : r + 1, :].astype(jnp.int32) == iota((half, cells), 0)
        found = dot(by_place, owner)
        for s in range(species):
            picked = jnp.where(place, found[s * half : (s + 1) * half, :], 0.0)
            picked = jnp.sum(picked, axis=0, keepdims=True)
            totals[s] = totals[s] + weight_ref[r : r + 1, :] * picked
    for s in range(species):
        bottom_ref[s : s + 1, :] = totals[s]


def whole():
    return pl.BlockSpec(memory_space=pltpu.VMEM)


def body(
    grad_columns,
    grad_flux,
    remap_part,
    remap_slot,
    remap_weight,
    col_count,
    neighbors,
    kappa,
    thickness,
    vertical,
    reaction,
):
    tiles, groups = lax.axis_size("tile"), lax.axis_size("spec")
    slots, width = grad_columns.shape
    species, layers = thickness.shape
    cells, per_cell = remap_part.shape
    rim = slots // 8
    outer = tiles // ROW
    digits = slots // RADIX
    nbr_count = neighbors.shape[1]
    dma = pltpu.SemaphoreType.DMA
    vmem = pltpu.VMEM
    grad_state, grad_bottom = pl.pallas_call(
        functools.partial(step_kernel, tiles, groups),
        out_shape=(
            vmem((slots, width), BF16),
            vmem((species, cells), F32),
        ),
        in_specs=[pl.BlockSpec(memory_space=pltpu.HBM)] * 11,
        out_specs=(whole(), whole()),
        scratch_shapes=[
            vmem((per_cell, cells), jnp.int32),
            vmem((per_cell, cells), jnp.int32),
            vmem((per_cell, cells), F32),
            vmem((species, cells), F32),
            vmem((slots, width), BF16),
            vmem((nbr_count, slots), jnp.int32),
            vmem((width, layers), BF16),
            vmem((species, layers), F32),
            vmem((1, 1), jnp.int32),
            vmem((1, species), F32),
            vmem((species, groups * species), BF16),
            vmem((per_cell, cells), F32),
            vmem((4 * tiles, width), F32),
            vmem((slots + 2 * rim, slots), BF16),
            vmem((slots, width), F32),
            vmem((width, width), BF16),
            vmem((groups * width, width), BF16),
            vmem((outer, ROW, 4, width), BF16),
            vmem((outer, ROW, 4, width), BF16),
            vmem((outer, ROW, 4, width), BF16),
            vmem((outer, ROW, 2, width), BF16),
            vmem((outer, ROW, 2, width), BF16),
            vmem((outer, ROW, 2, width), BF16),
            vmem((SUB, 2 * rim, width), BF16),
            vmem((SUB, 2 * rim, width), BF16),
            vmem((groups, slots, width), BF16),
            vmem((groups, digits, width), BF16),
            vmem((outer, digits, ROW // 2 * width), BF16),
            vmem((2 * rim, width), F32),
            vmem((2 * rim, width), F32),
            dma((11,)),
            dma((SUB, 2)),
            dma((SUB, 2)),
            dma((6,)),
            dma((6,)),
            dma((groups - 1,)),
            dma((groups - 1,)),
            dma((2, ROW - 1)),
            dma((2, ROW - 1)),
            dma((2, outer - 1)),
            dma((2, outer - 1)),
            dma((2, 2)),
        ],
        compiler_params=pltpu.CompilerParams(
            collective_id=0, has_side_effects=True, vmem_limit_bytes=60 * 2**20
        ),
        name="step",
    )(
        remap_part.T,
        remap_slot.T,
        remap_weight.T,
        grad_flux,
        grad_columns,
        neighbors.T,
        vertical.reshape(width, layers),
        thickness,
        col_count.reshape(1, 1),
        kappa.reshape(1, species),
        reaction.T,
    )
    return (grad_state, grad_bottom)


def solution(mesh):
    placed = (
        P("tile", "spec"),
        P("spec", "tile"),
        P("tile", None),
        P("tile", None),
        P("tile", None),
        P("tile"),
        P("tile", None),
        P("spec"),
        P("spec", None),
        P("spec", None, None),
        P(None, "spec"),
    )
    return jax.shard_map(
        body,
        mesh=mesh,
        in_specs=placed,
        out_specs=(P("tile", "spec"), P("spec", "tile")),
        check_vma=False,
    )
```
